256 devices in a mesh: tile: 32 (over x, y, core), mode: 8 (over z).
Axes of the slice: x: 4, y: 4, z: 8, core: 2. Of those that a mesh axis runs over, the one named last changes fastest.
Arguments:
- mode_shapes: bfloat16 [64, 256, 2048], P('mode', 'tile'), may hold values from -6 to 6
- stiffness: float32 [256, 2048], P('tile'), may hold values from 0.5 to 4
- node_slot: int32 [256, 2048], P('tile'), may hold values from 0 to 255, as said below
- slot_zone: int32 [32, 32, 8], replicated, may hold values from 0 to 15, as said below
Outputs:
- energy: float32 [512, 64, 64], P('tile', 'mode')
The draws below stay inside these ranges and needn't reach their ends.
Inputs may be any that keep to these rules, and one draw needn't show every extreme that they name: `slot_zone`: for each tile and owner, the 8 zone numbers are distinct. `node_slot`: slots that no node of a tile names carry no zone's nodes.
All inputs are finite; a program needn't handle non-finite values.
Results may differ from the reference program's by a relative error of at most 0.00099.
Values may be sent and summed in bfloat16 or wider, within the bound.
No kernel may reach another device: no remote copies, remote signals or barrier semaphores. Data moves between devices by JAX's collectives and lax.ppermute only.
A program may use at most 64 MiB of HBM per device.

```python
import math
import jax
import jax.numpy as jnp
from jax import lax

MODES = 64
ZONES = 512
CAP = 8
RX = 8
NY = 2048
NX = 256
ZONE_DEV = 16
SLOTS = 256
N_TILE = 32


def draw_node_slot(key, part):
    key_counts = jax.random.fold_in(key, 11)
    key_owner = jax.random.fold_in(key, 12)
    key_entry = jax.random.fold_in(key, 13)
    counts = jax.random.randint(key_counts, (N_TILE, N_TILE), 1, CAP + 1)
    counts = counts.at[:, N_TILE - 1].set(CAP)
    owner_tile = jax.random.randint(key_owner, (NX, NY), 0, N_TILE)
    entry_bits = jax.random.randint(key_entry, (NX, NY), 0, 1 << 20)
    tile_of = jnp.arange(NX) // RX
    live_count = counts[tile_of[:, None], owner_tile]
    slot_ids = owner_tile * CAP + entry_bits % live_count
    row_place = jnp.arange(NX)[:, None] % RX
    column_place = jnp.arange(NY)[None, :]
    slot_ids = jnp.where((row_place == RX - 1) & (column_place == NY - 1), SLOTS - 1, slot_ids)
    slot_ids = jnp.where((row_place == 0) & (column_place == 0), 0, slot_ids)
    return slot_ids.astype(jnp.int32)


def draw_slot_zone(key, part):
    key_scores = jax.random.fold_in(key, 21)
    scores = jax.random.randint(key_scores, (N_TILE, N_TILE, ZONE_DEV), 0, 1 << 16) * ZONE_DEV + jnp.arange(ZONE_DEV)
    ordering = jnp.argsort(scores, axis=-1, stable=True)
    return ordering[:, :, :CAP].astype(jnp.int32)


def block_levels(key, dims, shards, low, largest):
    level = 1.0
    for position, blocks in shards:
        heights = jax.random.uniform(jax.random.fold_in(jax.random.fold_in(key, 6), position), (blocks,), jnp.float32, low / len(shards), largest / len(shards))
        level = level * jnp.repeat(jnp.exp(heights), dims[position] // blocks).reshape((-1,) + (1,) * (len(dims) - 1 - position))
    return level


def scatter_about(rng, dims, deviation, reach, split=(), held_as=jnp.bfloat16):
    drawn = deviation * jax.random.normal(rng, dims, jnp.float32)
    if split:
        drawn = drawn * block_levels(rng, dims, split, -0.22, 0.18)
    return jnp.clip(drawn, -reach, reach).astype(held_as)


def setup_inputs(seed: int = 0) -> dict:
    key_list = jax.random.split(jax.random.key(seed), 5)
    return {
        "mode_shapes": scatter_about(key_list[0], (MODES, NX, NY), 1.0, 6.0, ((0, 8), (1, 32))),
        "stiffness": jnp.clip(jnp.exp(math.log(4.0) - 2.0794415 * jax.random.uniform(key_list[1], (NX, NY), jnp.float32) ** block_levels(key_list[1], (NX, NY), ((0, 32),), -0.2, 0.2)), 0.5, 4.0),
        "node_slot": draw_node_slot(jax.random.fold_in(key_list[4], 71), 0),
        "slot_zone": draw_slot_zone(jax.random.fold_in(key_list[4], 71), 0),
    }


POISSON = 0.3
SHEAR = 2.0 * (1.0 - POISSON)

def curvatures(shapes_framed):
    framed = jnp.pad(shapes_framed, ((0, 0), (0, 0), (1, 1)))
    centre = framed[:, 1:-1, 1:-1]
    along_x = framed[:, 2:, 1:-1] - 2.0 * centre + framed[:, :-2, 1:-1]
    along_y = framed[:, 1:-1, 2:] - 2.0 * centre + framed[:, 1:-1, :-2]
    twist_xy = 0.25 * (framed[:, 2:, 2:] - framed[:, 2:, :-2] - framed[:, :-2, 2:] + framed[:, :-2, :-2])
    return jnp.stack([along_x, along_y, twist_xy]).astype(jnp.bfloat16)

def left_factor(bending, stiffness):
    along_x, along_y, twist_xy = (bending[0], bending[1], bending[2])
    return jnp.stack([stiffness * (along_x + POISSON * along_y), stiffness * (along_y + POISSON * along_x), stiffness * (SHEAR * twist_xy)])

def reference(mode_shapes, stiffness, node_slot, slot_zone):
    framed = jnp.pad(mode_shapes.astype(jnp.float32), ((0, 0), (1, 1), (0, 0)))
    bending = lax.optimization_barrier(curvatures(framed)).astype(jnp.float32)
    weighted = left_factor(bending, stiffness)
    totals = 0.5 * lax.optimization_barrier(jnp.sum(weighted * bending, axis=(0, 2, 3)))
    left_round = lax.optimization_barrier(weighted.astype(jnp.bfloat16)).astype(jnp.float32)
    node_total = NX * NY
    left_flat = left_round.reshape(3, MODES, node_total)
    right_flat = bending.reshape(3, MODES, node_total)
    tile_of = jnp.arange(NX, dtype=jnp.int32) // RX
    owner_tile = node_slot // CAP
    within = node_slot % CAP
    zone_ids = (owner_tile * ZONE_DEV + slot_zone[tile_of[:, None], owner_tile, within]).reshape(node_total)
    block_nodes = math.gcd(node_total, 2048)

    def one_block(number, running):
        first_node = number * block_nodes
        left_block = lax.dynamic_slice_in_dim(left_flat, first_node, block_nodes, 2)
        right_block = lax.dynamic_slice_in_dim(right_flat, first_node, block_nodes, 2)
        zone_block = lax.dynamic_slice_in_dim(zone_ids, first_node, block_nodes, 0)
        outer_terms = jnp.einsum('cin,cjn->nij', left_block, right_block, precision=lax.Precision.HIGHEST)
        return running + jax.ops.segment_sum(outer_terms, zone_block, num_segments=ZONES)
    summed = lax.fori_loop(0, node_total // block_nodes, one_block, jnp.zeros((ZONES, MODES, MODES), jnp.float32))
    return ZONES * (0.5 * summed) / jnp.sqrt(totals[:, None] * totals[None, :])
```

```python
import functools

import jax
import jax.numpy as jnp
from jax import lax
from jax.experimental import pallas as pl
from jax.experimental.pallas import tpu as pltpu
from jax.sharding import PartitionSpec as P

ZONES = 512
POISSON = 0.3
SHEAR = 2.0 * (1.0 - POISSON)
CHUNK = 512

f32 = jnp.float32
bf16 = jnp.bfloat16


def stencil(shapes, stiff, cross, second, bend_out, left_out, total_out):
    framed_rows, modes, cells = shapes.shape
    lane = lax.broadcasted_iota(jnp.int32, (modes, cells), 1)

    def across(r, carry):
        w = shapes[r].astype(f32)
        right = jnp.where(lane == cells - 1, 0.0, pltpu.roll(w, cells - 1, 1))
        left = jnp.where(lane == 0, 0.0, pltpu.roll(w, 1, 1))
        cross[r] = right - left
        second[r] = (right - 2.0 * w) + left
        return carry

    lax.fori_loop(0, framed_rows, across, 0)

    def along(r, total):
        w = shapes[r + 1].astype(f32)
        along_x = (shapes[r + 2].astype(f32) - 2.0 * w) + shapes[r].astype(f32)
        bent = [along_x, second[r + 1], 0.25 * (cross[r + 2] - cross[r])]
        rounded = [b.astype(bf16) for b in bent]
        bx, by, bt = [b.astype(f32) for b in rounded]
        s = jnp.broadcast_to(stiff[pl.ds(r, 1), :], (modes, cells))
        weighted = [s * (bx + POISSON * by), s * (by + POISSON * bx), s * (SHEAR * bt)]
        for c in range(3):
            bend_out[c, r] = rounded[c]
            if left_out is not None:
                left_out[c, r] = weighted[c].astype(bf16)
        if total_out is None:
            return total
        energy = weighted[0] * bx + weighted[1] * by + weighted[2] * bt
        for k in range(cells // 128):
            total = total + energy[:, k * 128 : (k + 1) * 128]
        return total

    total = lax.fori_loop(0, framed_rows - 2, along, jnp.zeros((modes, 128), f32))
    if total_out is not None:
        total_out[...] = jnp.broadcast_to(jnp.sum(total, axis=1, keepdims=True), (modes, 128))


def pair_sums(slot, blocks, rows_scratch, acc):
    rows, cells = slot.shape
    slots = acc.shape[0]
    per_row = cells // CHUNK
    acc[...] = jnp.zeros_like(acc)
    slot_id = lax.broadcasted_iota(jnp.int32, (slots, CHUNK), 0).astype(f32).astype(bf16)

    def step(n, carry):
        r = n // per_row
        first = pl.multiple_of((n % per_row) * CHUNK, CHUNK)
        here = slot[pl.ds(r, 1), pl.ds(first, CHUNK)].astype(f32).astype(bf16)
        member = jnp.where(
            jnp.broadcast_to(here, (slots, CHUNK)) == slot_id,
            jnp.ones((slots, CHUNK), bf16),
            jnp.zeros((slots, CHUNK), bf16),
        )
        high, low = [], []
        for index, (left, bend) in enumerate(blocks):
            modes = left.shape[2]
            for c in range(3):
                rows_scratch[index, c] = left[c, r, :, pl.ds(first, CHUNK)].astype(f32)
            right = [bend[c, r, :, pl.ds(first, CHUNK)].astype(f32) for c in range(3)]
            for i in range(0, modes, 2):
                pair = []
                for k in (i, i + 1):
                    spread = [
                        jnp.broadcast_to(rows_scratch[index, c, pl.ds(k, 1), :], (modes, CHUNK))
                        for c in range(3)
                    ]
                    pair.append(spread[0] * right[0] + spread[1] * right[1] + spread[2] * right[2])
                product = jnp.concatenate(pair, axis=0)
                top = product.astype(bf16)
                high.append(top)
                low.append((product - top.astype(f32)).astype(bf16))
        contract = (((1,), (1,)), ((), ()))
        acc[...] += lax.dot_general(
            member, jnp.concatenate(high, axis=0), contract, preferred_element_type=f32
        ) + lax.dot_general(
            member, jnp.concatenate(low, axis=0), contract, preferred_element_type=f32
        )
        return carry

    lax.fori_loop(0, rows * per_row, step, 0)


def stage_own(shapes, stiff, slot, bend, left, total, sums, cross, second, rows_scratch):
    stencil(shapes, stiff, cross, second, bend, left, total)
    pair_sums(slot, [(left, bend)], rows_scratch, sums)


def stage_near(
    below, above, stiff, slot, bend, left,
    bend_below, left_below, total_below, bend_above, left_above, total_above, sums,
    cross, second, rows_scratch,
):
    stencil(below, stiff, cross, second, bend_below, left_below, total_below)
    stencil(above, stiff, cross, second, bend_above, left_above, total_above)
    blocks = [(left_below, bend_above), (left_above, bend_below), (left, bend_above), (left, bend_below)]
    pair_sums(slot, blocks, rows_scratch, sums)


def stage_far(
    below, above, stiff, slot, left_below, left_above,
    total, total_below, total_above, own_sums, near_sums,
    message,
    bend_far_below, left_far_below, bend_far_above, total_far_below, total_far_above,
    cross, second, rows_scratch, sums,
):
    stencil(below, stiff, cross, second, bend_far_below, left_far_below, total_far_below)
    stencil(above, stiff, cross, second, bend_far_above, None, total_far_above)
    blocks = [(left_below, bend_far_above), (left_above, bend_far_below), (left_far_below, bend_far_above)]
    pair_sums(slot, blocks, rows_scratch, sums)
    owners, entries, _ = message.shape
    message[:, :, 0:256] = near_sums[...].reshape(owners, entries, 256)
    message[:, :, 256:384] = sums[:, 0:128].reshape(owners, entries, 128)
    message[:, :, 384:512] = jnp.concatenate([sums[:, 128:192], own_sums[...]], axis=1).reshape(
        owners, entries, 128
    )
    lane = lax.broadcasted_iota(jnp.int32, total.shape, 1)
    panels = [total, total_above, total_far_above, total_far_below, total_below]
    places = jnp.zeros(total.shape, f32)
    for place, panel in enumerate(panels):
        places = jnp.where(lane == place, panel[...], places)
    message[:, :, 512:640] = jnp.broadcast_to(places[None], (owners, entries, 128))


def three_parts(x):
    a = x.astype(bf16)
    rest = x - a.astype(f32)
    b = rest.astype(bf16)
    return a, b, (rest - b.astype(f32)).astype(bf16)


def exact_dot(x, y, parts_of_y):
    if parts_of_y:
        return sum(jnp.dot(x, part, preferred_element_type=f32) for part in three_parts(y))
    return sum(jnp.dot(part, y, preferred_element_type=f32) for part in three_parts(x))


def gather_zones(received, lists, zoned):
    places, width = received.shape
    zones = zoned.shape[0] - 8
    body = width - 128
    chosen = jnp.broadcast_to(lists[...], (zones, places)) == lax.broadcasted_iota(
        jnp.int32, (zones, places), 0
    )
    chosen = jnp.where(chosen, 1.0, 0.0).astype(bf16)
    zoned[0:zones, :] = exact_dot(chosen, received[:, 0:body], True)
    totals = jnp.sum(received[:, body:].reshape(places // 8, 8, 128), axis=0)
    zoned[zones:, :] = jnp.concatenate([totals, jnp.zeros((8, body - 128), f32)], axis=1)


def normalise(place, mine, from_above, from_below, from_far, energy):
    zones = energy.shape[0]
    z = slice(0, zones)
    t = slice(zones, zones + 8)
    sums = jnp.concatenate(
        [
            mine[z, 448:512], mine[z, 128:192], from_above[z, 0:64], from_above[z, 256:320],
            from_far[z, 384:448], from_below[z, 320:384], from_below[z, 64:128], mine[z, 192:256],
        ],
        axis=1,
    )
    own = mine[t, 0:128]
    columns = [
        own[:, 0:1], own[:, 1:2], own[:, 2:3], from_above[t, 2:3],
        from_far[t, 2:3], from_below[t, 3:4], own[:, 3:4], own[:, 4:5],
    ]
    spread = jnp.concatenate([jnp.broadcast_to(c, (8, 64)) for c in columns], axis=1)
    sub = lax.broadcasted_iota(jnp.int32, (8, 512), 0)
    lane = lax.broadcasted_iota(jnp.int32, (8, 512), 1)
    total_j = jnp.sum(jnp.where(lane % 8 == sub, spread, 0.0), axis=0, keepdims=True)
    total_i = jnp.sum(
        jnp.where((lane // 8) % 8 == sub, jnp.broadcast_to(own[:, 0:1], (8, 512)), 0.0), axis=0, keepdims=True
    )
    scaled = ZONES * (0.5 * sums) / jnp.sqrt((0.5 * total_i) * (0.5 * total_j))
    r = lax.broadcasted_iota(jnp.int32, (512, 512), 0)
    c = lax.broadcasted_iota(jnp.int32, (512, 512), 1)
    panel = (r // 64 + place[0]) % 8
    target = ((r // 8) % 8) * 64 + panel * 8 + r % 8
    order = jnp.where(c == target, 1.0, 0.0).astype(bf16)
    ordered = exact_dot(scaled, order, False)
    for i in range(8):
        energy[:, i, :] = ordered[:, i * 64 : (i + 1) * 64]


def vmem(shape, dtype=f32):
    return pltpu.VMEM(shape, dtype)


def call(body, outs, scratch, *args, scalars=0):
    specs = [pl.BlockSpec(memory_space=pltpu.SMEM)] * scalars + [
        pl.BlockSpec(memory_space=pltpu.VMEM)
    ] * (len(args) - scalars)
    return pl.pallas_call(
        body,
        out_shape=[jax.ShapeDtypeStruct(s, d) for s, d in outs],
        in_specs=specs,
        out_specs=[pl.BlockSpec(memory_space=pltpu.VMEM)] * len(outs),
        scratch_shapes=scratch,
        name=body.__name__,
    )(*args)


def per_device(mode_shapes, stiffness, node_slot, slot_zone):
    modes, rows, cells = mode_shapes.shape
    tiles = lax.axis_size("tile")
    panels = lax.axis_size("mode")
    entries = slot_zone.shape[2]
    slots = tiles * entries
    owned = ZONES // tiles
    up = [(i, i + 1) for i in range(tiles - 1)]
    down = [(i + 1, i) for i in range(tiles - 1)]

    def turn(x, by):
        return lax.ppermute(x, "mode", [(i, (i + by) % panels) for i in range(panels)])

    head = lax.ppermute(mode_shapes[:, rows - 1], "tile", up)
    tail = lax.ppermute(mode_shapes[:, 0], "tile", down)
    framed = jnp.concatenate([head[None], jnp.transpose(mode_shapes, (1, 0, 2)), tail[None]], axis=0)
    below = turn(framed, 1)
    above = turn(framed, -1)
    far_below = turn(below, 1)
    far_above = turn(above, -1)

    factor = ((3, rows, modes, cells), bf16)
    total = ((modes, 128), f32)
    lines = [vmem((rows + 2, modes, cells)), vmem((rows + 2, modes, cells))]
    pairs = modes * modes
    bend0, left0, total0, own_sums = call(
        stage_own, [factor, factor, total, ((slots, pairs), f32)],
        lines + [vmem((1, 3, modes, CHUNK))],
        framed, stiffness, node_slot,
    )
    _, left_below, total_below, _, left_above, total_above, near_sums = call(
        stage_near, [factor, factor, total, factor, factor, total, ((slots, 4 * pairs), f32)],
        lines + [vmem((4, 3, modes, CHUNK))],
        below, above, stiffness, node_slot, bend0, left0,
    )
    (message,) = call(
        stage_far, [((tiles, entries, 8 * pairs + 128), f32)],
        [vmem(*factor), vmem(*factor), vmem(*factor), vmem(*total), vmem(*total)]
        + lines + [vmem((3, 3, modes, CHUNK)), vmem((slots, 3 * pairs))],
        far_below, far_above, stiffness, node_slot, left_below, left_above,
        total0, total_below, total_above, own_sums, near_sums,
    )
    received = lax.all_to_all(message, "tile", 0, 0, tiled=True)
    lists = lax.dynamic_index_in_dim(slot_zone, lax.axis_index("tile"), 1, keepdims=False)
    (zoned,) = call(
        gather_zones, [((owned + 8, 8 * pairs), f32)], [],
        received.reshape(slots, 8 * pairs + 128), lists.reshape(1, slots),
    )
    from_above = turn(zoned, -1)
    from_below = turn(zoned, 1)
    from_far = turn(zoned, -2)
    place = lax.axis_index("mode").astype(jnp.int32).reshape(1)
    (energy,) = call(
        normalise, [((owned, modes, panels * modes), f32)], [],
        place, zoned, from_above, from_below, from_far, scalars=1,
    )
    return energy


def solution(mesh):
    placed = (P("mode", "tile", None), P("tile", None), P("tile", None), P())
    return jax.shard_map(
        per_device, mesh=mesh, in_specs=placed, out_specs=P("tile", "mode", None), check_vma=False
    )
```

```python
import jax
import jax.numpy as jnp
from jax import lax
from jax.experimental import pallas as pl
from jax.experimental.pallas import tpu as pltpu
from jax.sharding import PartitionSpec as P


ZONES = 512
POISSON = 0.3
SHEAR = 2.0 * (1.0 - POISSON)
CHUNK = 512
MERGE = 4

f32 = jnp.float32
bf16 = jnp.bfloat16


def stencil(shapes, stiff, plain, cross, second, bend_out, left_out, total_out):
    framed_rows, modes, cells = shapes.shape
    lane = lax.broadcasted_iota(jnp.int32, (modes, cells), 1)
    group = 5

    def across(n, carry):
        for k in range(group):
            r = n * group + k
            w = shapes[r].astype(f32)
            right = jnp.where(lane == cells - 1, 0.0, pltpu.roll(w, cells - 1, 1))
            left = jnp.where(lane == 0, 0.0, pltpu.roll(w, 1, 1))
            plain[r] = w
            cross[r] = right - left
            second[r] = (right - 2.0 * w) + left
        return carry

    lax.fori_loop(0, framed_rows // group, across, 0)

    def along(r, total):
        along_x = (plain[r + 2] - 2.0 * plain[r + 1]) + plain[r]
        bent = [along_x, second[r + 1], 0.25 * (cross[r + 2] - cross[r])]
        rounded = [b.astype(bf16) for b in bent]
        bx, by, bt = [b.astype(f32) for b in rounded]
        s = jnp.broadcast_to(stiff[pl.ds(r, 1), :], (modes, cells))
        weighted = [s * (bx + POISSON * by), s * (by + POISSON * bx), s * (SHEAR * bt)]
        for c in range(3):
            bend_out[c, r] = rounded[c]
            if left_out is not None:
                left_out[c, r] = weighted[c].astype(bf16)
        energy = weighted[0] * bx + weighted[1] * by + weighted[2] * bt
        for k in range(cells // 128):
            total = total + energy[:, k * 128 : (k + 1) * 128]
        return total

    total = lax.fori_loop(0, framed_rows - 2, along, jnp.zeros((modes, 128), f32))
    total_out[...] = jnp.broadcast_to(jnp.sum(total, axis=1, keepdims=True), (modes, 128))


def pair_sums(slot, lefts, bends, blocks, wide, acc):
    rows, cells = slot.shape
    slots, width = acc.shape
    pairs = bends[0].shape[2] ** 2
    narrow = width == 2 * len(blocks) * pairs
    acc[...] = jnp.zeros_like(acc)
    slot_id = lax.broadcasted_iota(jnp.int32, (slots, CHUNK), 0).astype(f32).astype(bf16)

    def widen(r, carry):
        for index, left in enumerate(lefts):
            for c in range(3):
                wide[index, c, r] = left[c, r].astype(f32)
        return carry

    lax.fori_loop(0, rows, widen, 0)

    def one_row(r, carry):
        for base in range(0, cells, CHUNK * MERGE):
            members, high, low = [], [], []
            for first in range(base, base + CHUNK * MERGE, CHUNK):
                cut = slice(first, first + CHUNK)
                here = slot[pl.ds(r, 1), cut].astype(f32).astype(bf16)
                members.append(
                    jnp.where(
                        jnp.broadcast_to(here, (slots, CHUNK)) == slot_id,
                        jnp.ones((slots, CHUNK), bf16),
                        jnp.zeros((slots, CHUNK), bf16),
                    )
                )
                top, rest = [], []
                for left, bend in blocks:
                    right = [bends[bend][c, r, :, cut].astype(f32) for c in range(3)]
                    modes = right[0].shape[0]
                    for i in range(0, modes, 2):
                        pair = []
                        for k in (i, i + 1):
                            spread = [
                                jnp.broadcast_to(wide[left, c, r, pl.ds(k, 1), cut], (modes, CHUNK))
                                for c in range(3)
                            ]
                            pair.append(
                                spread[0] * right[0] + spread[1] * right[1] + spread[2] * right[2]
                            )
                        product = jnp.concatenate(pair, axis=0)
                        top.append(product.astype(bf16))
                        rest.append((product - top[-1].astype(f32)).astype(bf16))
                high.append(jnp.concatenate(top, axis=0))
                low.append(jnp.concatenate(rest, axis=0))
            if narrow:
                member = jnp.concatenate(members, axis=1)
                product = jnp.concatenate(
                    [jnp.concatenate(high, axis=1), jnp.concatenate(low, axis=1)], axis=0
                )
            else:
                member = jnp.concatenate(members + members, axis=1)
                product = jnp.concatenate(high + low, axis=1)
            acc[...] += lax.dot_general(
                member, product, (((1,), (1,)), ((), ())), preferred_element_type=f32
            )
        return carry

    lax.fori_loop(0, rows, one_row, 0)


def stage_own(shapes, stiff, slot, bend, left, total, sums, plain, cross, second, wide, acc):
    stencil(shapes, stiff, plain, cross, second, bend, left, total)
    pair_sums(slot, [left], [bend], [(0, 0)], wide, acc)
    pairs = sums.shape[1]
    sums[...] = acc[:, 0:pairs] + acc[:, pairs : 2 * pairs]


def stage_near(
    below, above, stiff, slot, bend, left,
    bend_below, left_below, total_below, bend_above, left_above, total_above, sums,
    plain, cross, second, wide,
):
    stencil(below, stiff, plain, cross, second, bend_below, left_below, total_below)
    stencil(above, stiff, plain, cross, second, bend_above, left_above, total_above)
    blocks = [(0, 1), (1, 0), (2, 1), (2, 0)]
    pair_sums(slot, [left_below, left_above, left], [bend_below, bend_above], blocks, wide, sums)


def stage_far(
    below, above, stiff, slot, left_below, left_above,
    total, total_below, total_above, own_sums, near_sums,
    message,
    bend_far_below, left_far_below, bend_far_above, total_far_below, total_far_above,
    plain, cross, second, sums, wide,
):
    stencil(below, stiff, plain, cross, second, bend_far_below, left_far_below, total_far_below)
    stencil(above, stiff, plain, cross, second, bend_far_above, None, total_far_above)
    lefts = [left_below, left_above, left_far_below]
    pair_sums(slot, lefts, [bend_far_below, bend_far_above], [(0, 1), (1, 0), (2, 1)], wide, sums)
    owners, entries, _ = message.shape
    message[:, :, 0:256] = near_sums[...].reshape(owners, entries, 256)
    message[:, :, 256:384] = sums[:, 0:128].reshape(owners, entries, 128)
    message[:, :, 384:512] = jnp.concatenate([sums[:, 128:192], own_sums[...]], axis=1).reshape(
        owners, entries, 128
    )
    lane = lax.broadcasted_iota(jnp.int32, total.shape, 1)
    panels = [total, total_above, total_far_above, total_far_below, total_below]
    places = jnp.zeros(total.shape, f32)
    for place, panel in enumerate(panels):
        places = jnp.where(lane == place, panel[...], places)
    message[:, :, 512:640] = jnp.broadcast_to(places[None], (owners, entries, 128))


def three_parts(x):
    a = x.astype(bf16)
    rest = x - a.astype(f32)
    b = rest.astype(bf16)
    return a, b, (rest - b.astype(f32)).astype(bf16)


def exact_dot(x, y, parts_of_y):
    if parts_of_y:
        return sum(jnp.dot(x, part, preferred_element_type=f32) for part in three_parts(y))
    return sum(jnp.dot(part, y, preferred_element_type=f32) for part in three_parts(x))


def gather_zones(received, lists, zoned):
    places, width = received.shape
    zones = zoned.shape[0] - 8
    body = width - 128
    chosen = jnp.broadcast_to(lists[...], (zones, places)) == lax.broadcasted_iota(
        jnp.int32, (zones, places), 0
    )
    chosen = jnp.where(chosen, 1.0, 0.0).astype(bf16)
    zoned[0:zones, :] = exact_dot(chosen, received[:, 0:body], True)
    totals = jnp.sum(received[:, body:].reshape(places // 8, 8, 128), axis=0)
    zoned[zones:, :] = jnp.concatenate([totals, jnp.zeros((8, body - 128), f32)], axis=1)


def normalise(place, mine, from_above, from_below, from_far, energy):
    zones = energy.shape[0]
    z = slice(0, zones)
    t = slice(zones, zones + 8)
    sums = jnp.concatenate(
        [
            mine[z, 448:512], mine[z, 128:192], from_above[z, 0:64], from_above[z, 256:320],
            from_far[z, 384:448], from_below[z, 320:384], from_below[z, 64:128], mine[z, 192:256],
        ],
        axis=1,
    )
    own = mine[t, 0:128]
    columns = [
        own[:, 0:1], own[:, 1:2], own[:, 2:3], from_above[t, 2:3],
        from_far[t, 2:3], from_below[t, 3:4], own[:, 3:4], own[:, 4:5],
    ]
    spread = jnp.concatenate([jnp.broadcast_to(c, (8, 64)) for c in columns], axis=1)
    sub = lax.broadcasted_iota(jnp.int32, (8, 512), 0)
    lane = lax.broadcasted_iota(jnp.int32, (8, 512), 1)
    total_j = jnp.sum(jnp.where(lane % 8 == sub, spread, 0.0), axis=0, keepdims=True)
    total_i = jnp.sum(
        jnp.where((lane // 8) % 8 == sub, jnp.broadcast_to(own[:, 0:1], (8, 512)), 0.0), axis=0, keepdims=True
    )
    scaled = ZONES * (0.5 * sums) / jnp.sqrt((0.5 * total_i) * (0.5 * total_j))
    r = lax.broadcasted_iota(jnp.int32, (512, 512), 0)
    c = lax.broadcasted_iota(jnp.int32, (512, 512), 1)
    panel = (r // 64 + place[0]) % 8
    target = ((r // 8) % 8) * 64 + panel * 8 + r % 8
    order = jnp.where(c == target, 1.0, 0.0).astype(bf16)
    ordered = exact_dot(scaled, order, False)
    for i in range(8):
        energy[:, i, :] = ordered[:, i * 64 : (i + 1) * 64]


def vmem(shape, dtype=f32):
    return pltpu.VMEM(shape, dtype)


def call(body, outs, scratch, *args, scalars=0):
    specs = [pl.BlockSpec(memory_space=pltpu.SMEM)] * scalars + [
        pl.BlockSpec(memory_space=pltpu.VMEM)
    ] * (len(args) - scalars)
    return pl.pallas_call(
        body,
        out_shape=[jax.ShapeDtypeStruct(s, d) for s, d in outs],
        in_specs=specs,
        out_specs=[pl.BlockSpec(memory_space=pltpu.VMEM)] * len(outs),
        scratch_shapes=scratch,
    )(*args)


def per_device(mode_shapes, stiffness, node_slot, slot_zone):
    modes, rows, cells = mode_shapes.shape
    tiles = lax.axis_size("tile")
    panels = lax.axis_size("mode")
    entries = slot_zone.shape[2]
    slots = tiles * entries
    owned = ZONES // tiles
    up = [(i, i + 1) for i in range(tiles - 1)]
    down = [(i + 1, i) for i in range(tiles - 1)]

    def turn(x, by):
        return lax.ppermute(x, "mode", [(i, (i + by) % panels) for i in range(panels)])

    head = lax.ppermute(mode_shapes[:, rows - 1], "tile", up)
    tail = lax.ppermute(mode_shapes[:, 0], "tile", down)
    framed = jnp.concatenate([head[None], jnp.transpose(mode_shapes, (1, 0, 2)), tail[None]], axis=0)
    below = turn(framed, 1)
    above = turn(framed, -1)
    far_below = turn(below, 1)
    far_above = turn(above, -1)

    lists = lax.dynamic_index_in_dim(slot_zone, lax.axis_index("tile"), 1, keepdims=False)
    lists = lists.reshape(1, slots)
    factor = ((3, rows, modes, cells), bf16)
    total = ((modes, 128), f32)
    lines = [vmem((rows + 2, modes, cells))] * 3
    pairs = modes * modes
    bend0, left0, total0, own_sums = call(
        stage_own, [factor, factor, total, ((slots, pairs), f32)],
        lines + [vmem((1, 3, rows, modes, cells)), vmem((slots, 2 * pairs))],
        framed, stiffness, node_slot,
    )
    _, left_below, total_below, _, left_above, total_above, near_sums = call(
        stage_near, [factor, factor, total, factor, factor, total, ((slots, 4 * pairs), f32)],
        lines + [vmem((3, 3, rows, modes, cells))],
        below, above, stiffness, node_slot, bend0, left0,
    )
    (message,) = call(
        stage_far, [((tiles, entries, 8 * pairs + 128), f32)],
        [vmem(*factor), vmem(*factor), vmem(*factor), vmem(*total), vmem(*total)]
        + lines + [vmem((slots, 3 * pairs)), vmem((3, 3, rows, modes, cells))],
        far_below, far_above, stiffness, node_slot, left_below, left_above,
        total0, total_below, total_above, own_sums, near_sums,
    )
    message, lists = lax.optimization_barrier((message, lists))
    received = lax.all_to_all(message, "tile", 0, 0, tiled=True)
    (zoned,) = call(
        gather_zones, [((owned + 8, 8 * pairs), f32)], [],
        received.reshape(slots, 8 * pairs + 128), lists,
    )
    from_above = turn(zoned, -1)
    from_below = turn(zoned, 1)
    from_far = turn(zoned, -2)
    place = lax.axis_index("mode").astype(jnp.int32).reshape(1)
    (energy,) = call(
        normalise, [((owned, modes, panels * modes), f32)], [],
        place, zoned, from_above, from_below, from_far, scalars=1,
    )
    return energy


def solution(mesh):
    placed = (P("mode", "tile", None), P("tile", None), P("tile", None), P())

    return jax.shard_map(per_device, mesh=mesh, in_specs=placed, out_specs=P("tile", "mode", None), check_vma=False)
```

```python
import jax
import jax.numpy as jnp
from jax import lax
from jax.experimental import pallas as pl
from jax.experimental.pallas import tpu as pltpu
from jax.sharding import PartitionSpec as P


ZONES = 512
POISSON = 0.3
SHEAR = 2.0 * (1.0 - POISSON)
CHUNK = 512

f32 = jnp.float32
bf16 = jnp.bfloat16


def stencil(shapes, stiff, lines, bend_out, left_out=None, total_out=None):
    framed_rows, modes, cells = shapes.shape
    plain, cross, second = lines
    lane = lax.broadcasted_iota(jnp.int32, (modes, cells), 1)
    group = 5

    def across(n, carry):
        for k in range(group):
            r = n * group + k
            w = shapes[r].astype(f32)
            right = jnp.where(lane == cells - 1, 0.0, pltpu.roll(w, cells - 1, 1))
            left = jnp.where(lane == 0, 0.0, pltpu.roll(w, 1, 1))
            plain[r] = w
            cross[r] = right - left
            second[r] = (right - 2.0 * w) + left
        return carry

    lax.fori_loop(0, framed_rows // group, across, 0)

    def along(r, total):
        along_x = (plain[r + 2] - 2.0 * plain[r + 1]) + plain[r]
        bent = [along_x, second[r + 1], 0.25 * (cross[r + 2] - cross[r])]
        bx, by, bt = [b.astype(bf16).astype(f32) for b in bent]
        for c, b in enumerate((bx, by, bt)):
            bend_out[c, r] = b
        if left_out is None and total_out is None:
            return total
        s = jnp.broadcast_to(stiff[pl.ds(r, 1), :], (modes, cells))
        weighted = [s * (bx + POISSON * by), s * (by + POISSON * bx), s * (SHEAR * bt)]
        if left_out is not None:
            for c in range(3):
                left_out[c, r] = weighted[c].astype(bf16).astype(f32)
        if total_out is None:
            return total
        energy = weighted[0] * bx + weighted[1] * by + weighted[2] * bt
        for k in range(cells // 128):
            total = total + energy[:, k * 128 : (k + 1) * 128]
        return total

    total = lax.fori_loop(0, framed_rows - 2, along, jnp.zeros((modes, 128), f32))
    if total_out is not None:
        total_out[...] = jnp.broadcast_to(jnp.sum(total, axis=1, keepdims=True), (modes, 128))


def pair_sums(slot, blocks, acc):
    rows, cells = slot.shape
    width, slots = acc.shape
    half = len(blocks) * blocks[0][0].shape[2] ** 2
    spare = [jnp.zeros((width - 2 * half, cells), bf16)] if width > 2 * half else []
    acc[...] = jnp.zeros_like(acc)
    slot_id = lax.broadcasted_iota(jnp.int32, (slots, CHUNK), 0).astype(f32).astype(bf16)

    def one_row(r, carry):
        members, high, low = [], [], []
        for first in range(0, cells, CHUNK):
            cut = slice(first, first + CHUNK)
            here = slot[pl.ds(r, 1), cut].astype(f32).astype(bf16)
            members.append(
                jnp.where(
                    jnp.broadcast_to(here, (slots, CHUNK)) == slot_id,
                    jnp.ones((slots, CHUNK), bf16),
                    jnp.zeros((slots, CHUNK), bf16),
                )
            )
            top, rest = [], []
            for left, bend in blocks:
                right = [bend[c, r, :, cut] for c in range(3)]
                modes = right[0].shape[0]
                for i in range(0, modes, 2):
                    pair = []
                    for k in (i, i + 1):
                        spread = [
                            jnp.broadcast_to(left[c, r, pl.ds(k, 1), cut], (modes, CHUNK))
                            for c in range(3)
                        ]
                        pair.append(spread[0] * right[0] + spread[1] * right[1] + spread[2] * right[2])
                    product = jnp.concatenate(pair, axis=0)
                    top.append(product.astype(bf16))
                    rest.append((product - top[-1].astype(f32)).astype(bf16))
            high.append(jnp.concatenate(top, axis=0))
            low.append(jnp.concatenate(rest, axis=0))
        products = jnp.concatenate(
            [jnp.concatenate(high, axis=1), jnp.concatenate(low, axis=1)] + spare, axis=0
        )
        acc[...] += lax.dot_general(
            products, jnp.concatenate(members, axis=1), (((1,), (1,)), ((), ())), preferred_element_type=f32
        )
        return carry

    lax.fori_loop(0, rows, one_row, 0, unroll=2)
    return jnp.transpose(acc[0:half, :] + acc[half : 2 * half, :])


def stage_own(shapes, stiff, slot, bend, left, total, sums, plain, cross, second, acc):
    stencil(shapes, stiff, (plain, cross, second), bend, left, total)
    sums[...] = pair_sums(slot, [(left, bend)], acc)


def stage_near(
    below, above, stiff, slot, bend, left,
    bend_above, left_above, total_above, sums,
    bend_below, plain, cross, second, acc,
):
    lines = (plain, cross, second)
    stencil(below, stiff, lines, bend_below)
    stencil(above, stiff, lines, bend_above, left_above, total_above)
    sums[...] = pair_sums(slot, [(left, bend_above), (left, bend_below)], acc)


def stage_far(
    below, above, stiff, slot, left, bend_above, left_above,
    total, total_above, own_sums, near_sums,
    message,
    bend_far_below, left_far_below, bend_far_above, total_far_below, total_far_above,
    plain, cross, second, acc,
):
    lines = (plain, cross, second)
    stencil(below, stiff, lines, bend_far_below, left_far_below, total_far_below)
    stencil(above, stiff, lines, bend_far_above, None, total_far_above)
    blocks = [
        (left, bend_far_above), (left, bend_far_below), (left_far_below, bend_above),
        (left_far_below, bend_far_above), (left_above, bend_far_below),
    ]
    sums = pair_sums(slot, blocks, acc)
    owners, entries, _ = message.shape
    message[:, :, 0:128] = near_sums[...].reshape(owners, entries, 128)
    message[:, :, 128:512] = jnp.concatenate([sums, own_sums[...]], axis=1).reshape(owners, entries, 384)
    lane = lax.broadcasted_iota(jnp.int32, total.shape, 1)
    places = jnp.zeros(total.shape, f32)
    for place, panel in enumerate([total, total_above, total_far_above, total_far_below]):
        places = jnp.where(lane == place, panel[...], places)
    message[:, :, 512:640] = jnp.broadcast_to(places[None], (owners, entries, 128))


def three_parts(x):
    a = x.astype(bf16)
    rest = x - a.astype(f32)
    b = rest.astype(bf16)
    return a, b, (rest - b.astype(f32)).astype(bf16)


def exact_dot(x, y, parts_of_y):
    if parts_of_y:
        return sum(jnp.dot(x, part, preferred_element_type=f32) for part in three_parts(y))
    return sum(jnp.dot(part, y, preferred_element_type=f32) for part in three_parts(x))


def gather_zones(received, lists, mine, to_far, to_next):
    places, width = received.shape
    zones = mine.shape[0]
    body = width - 128
    chosen = jnp.broadcast_to(lists[...], (zones, places)) == lax.broadcasted_iota(
        jnp.int32, (zones, places), 0
    )
    chosen = jnp.where(chosen, 1.0, 0.0).astype(bf16)
    zoned = exact_dot(chosen, received[:, 0:body], True)
    totals = jnp.sum(received[:, body:].reshape(places // 8, 8, 128), axis=0)
    mine[...] = zoned[:, 0:256]
    to_far[0:zones, :] = zoned[:, 256:384]
    to_far[zones:, :] = totals
    to_next[0:zones, :] = zoned[:, 384:512]
    to_next[zones:, :] = totals


def normalise(place, mine, kept, from_far, from_below, energy):
    zones = energy.shape[0]
    z = slice(0, zones)
    t = slice(zones, zones + 8)
    sums = jnp.concatenate(
        [
            kept[z, 64:128], mine[:, 0:64], mine[:, 128:192], from_far[z, 0:64],
            from_far[z, 64:128], from_below[z, 0:64], mine[:, 192:256], mine[:, 64:128],
        ],
        axis=1,
    )
    own, far, below = kept[t, :], from_far[t, :], from_below[t, :]
    columns = [
        own[:, 0:1], own[:, 1:2], own[:, 2:3], far[:, 1:2],
        far[:, 2:3], below[:, 3:4], own[:, 3:4], below[:, 0:1],
    ]
    spread = jnp.concatenate([jnp.broadcast_to(c, (8, 64)) for c in columns], axis=1)
    sub = lax.broadcasted_iota(jnp.int32, (8, 512), 0)
    lane = lax.broadcasted_iota(jnp.int32, (8, 512), 1)
    total_j = jnp.sum(jnp.where(lane % 8 == sub, spread, 0.0), axis=0, keepdims=True)
    total_i = jnp.sum(
        jnp.where((lane // 8) % 8 == sub, jnp.broadcast_to(own[:, 0:1], (8, 512)), 0.0), axis=0, keepdims=True
    )
    scaled = ZONES * (0.5 * sums) / jnp.sqrt((0.5 * total_i) * (0.5 * total_j))
    r = lax.broadcasted_iota(jnp.int32, (512, 512), 0)
    c = lax.broadcasted_iota(jnp.int32, (512, 512), 1)
    panel = (r // 64 + place[0]) % 8
    target = ((r // 8) % 8) * 64 + panel * 8 + r % 8
    order = jnp.where(c == target, 1.0, 0.0).astype(bf16)
    ordered = exact_dot(scaled, order, False)
    for i in range(8):
        energy[:, i, :] = ordered[:, i * 64 : (i + 1) * 64]


def vmem(shape, dtype=f32):
    return pltpu.VMEM(shape, dtype)


def call(body, outs, scratch, *args, scalars=0):
    specs = [pl.BlockSpec(memory_space=pltpu.SMEM)] * scalars + [
        pl.BlockSpec(memory_space=pltpu.VMEM)
    ] * (len(args) - scalars)
    return pl.pallas_call(
        body,
        out_shape=[jax.ShapeDtypeStruct(s, d) for s, d in outs],
        in_specs=specs,
        out_specs=[pl.BlockSpec(memory_space=pltpu.VMEM)] * len(outs),
        scratch_shapes=scratch,
        compiler_params=pltpu.CompilerParams(vmem_limit_bytes=24 << 20),
    )(*args)


def per_device(mode_shapes, stiffness, node_slot, slot_zone):
    modes, rows, cells = mode_shapes.shape
    tiles = lax.axis_size("tile")
    panels = lax.axis_size("mode")
    entries = slot_zone.shape[2]
    slots = tiles * entries
    owned = ZONES // tiles
    up = [(i, i + 1) for i in range(tiles - 1)]
    down = [(i + 1, i) for i in range(tiles - 1)]

    def turn(x, by):
        return lax.ppermute(x, "mode", [(i, (i + by) % panels) for i in range(panels)])

    lists = lax.dynamic_index_in_dim(slot_zone, lax.axis_index("tile"), 1, keepdims=False)
    lists = lists.reshape(1, slots)
    head = lax.ppermute(mode_shapes[:, rows - 1], "tile", up)
    tail = lax.ppermute(mode_shapes[:, 0], "tile", down)
    framed = jnp.concatenate([head[None], jnp.transpose(mode_shapes, (1, 0, 2)), tail[None]], axis=0)
    framed, lists = lax.optimization_barrier((framed, lists))
    below = turn(framed, 1)
    above = turn(framed, -1)
    far_below = turn(below, 1)
    far_above = turn(above, -1)

    factor = ((3, rows, modes, cells), f32)
    total = ((modes, 128), f32)
    lines = [vmem((rows + 2, modes, cells))] * 3
    pairs = modes * modes
    bend0, left0, total0, own_sums = call(
        stage_own, [factor, factor, total, ((slots, pairs), f32)],
        lines + [vmem((2 * pairs, slots))],
        framed, stiffness, node_slot,
    )
    bend_above, left_above, total_above, near_sums = call(
        stage_near, [factor, factor, total, ((slots, 2 * pairs), f32)],
        [vmem(*factor)] + lines + [vmem((4 * pairs, slots))],
        below, above, stiffness, node_slot, bend0, left0,
    )
    (message,) = call(
        stage_far, [((tiles, entries, 8 * pairs + 128), f32)],
        [vmem(*factor)] * 3 + [vmem(*total)] * 2 + lines + [vmem((10 * pairs, slots))],
        far_below, far_above, stiffness, node_slot, left0, bend_above, left_above,
        total0, total_above, own_sums, near_sums,
    )
    message, lists = lax.optimization_barrier((message, lists))
    received = lax.all_to_all(message, "tile", 0, 0, tiled=True)
    mine, to_far, to_next = call(
        gather_zones,
        [((owned, 4 * pairs), f32), ((owned + 8, 2 * pairs), f32), ((owned + 8, 2 * pairs), f32)], [],
        received.reshape(slots, 8 * pairs + 128), lists,
    )
    from_far = turn(to_far, -2)
    from_below = turn(to_next, 1)
    place = lax.axis_index("mode").astype(jnp.int32).reshape(1)
    (energy,) = call(
        normalise, [((owned, modes, panels * modes), f32)], [],
        place, mine, to_next, from_far, from_below, scalars=1,
    )
    return energy


def solution(mesh):
    placed = (P("mode", "tile", None), P("tile", None), P("tile", None), P())

    return jax.shard_map(per_device, mesh=mesh, in_specs=placed, out_specs=P("tile", "mode", None), check_vma=False)
```

```python
import jax
import jax.numpy as jnp
from jax import lax
from jax.experimental import pallas as pl
from jax.experimental.pallas import tpu as pltpu
from jax.sharding import PartitionSpec as P


ZONES = 512
POISSON = 0.3
SHEAR = 2.0 * (1.0 - POISSON)
CHUNK = 512

f32 = jnp.float32
bf16 = jnp.bfloat16


def stencil(panel, stiff, lines, bend_out, left_out=None, total_out=None):
    body, edge = panel
    rows, modes, cells = body.shape
    plain, cross, second = lines
    lane = lax.broadcasted_iota(jnp.int32, (modes, cells), 1)
    group = 4

    def across(r, w):
        right = jnp.where(lane == cells - 1, 0.0, pltpu.roll(w, cells - 1, 1))
        left = jnp.where(lane == 0, 0.0, pltpu.roll(w, 1, 1))
        plain[r] = w
        cross[r] = right - left
        second[r] = (right - 2.0 * w) + left

    def some_rows(n, carry):
        for k in range(group):
            across(n * group + k + 1, body[n * group + k].astype(f32))
        return carry

    across(0, edge[0].astype(f32))
    across(rows + 1, edge[1].astype(f32))
    lax.fori_loop(0, rows // group, some_rows, 0)

    def along(r, total):
        along_x = (plain[r + 2] - 2.0 * plain[r + 1]) + plain[r]
        bent = [along_x, second[r + 1], 0.25 * (cross[r + 2] - cross[r])]
        bx, by, bt = [b.astype(bf16).astype(f32) for b in bent]
        for c, b in enumerate((bx, by, bt)):
            bend_out[c, r] = b
        if left_out is None and total_out is None:
            return total
        s = jnp.broadcast_to(stiff[pl.ds(r, 1), :], (modes, cells))
        weighted = [s * (bx + POISSON * by), s * (by + POISSON * bx), s * (SHEAR * bt)]
        if left_out is not None:
            for c in range(3):
                left_out[c, r] = weighted[c].astype(bf16).astype(f32)
        if total_out is None:
            return total
        energy = weighted[0] * bx + weighted[1] * by + weighted[2] * bt
        for k in range(cells // 128):
            total = total + energy[:, k * 128 : (k + 1) * 128]
        return total

    total = lax.fori_loop(0, rows, along, jnp.zeros((modes, 128), f32))
    if total_out is not None:
        total_out[...] = jnp.broadcast_to(jnp.sum(total, axis=1, keepdims=True), (modes, 128))


def pair_sums(slot, blocks, acc):
    rows, cells = slot.shape
    width, slots = acc.shape
    half = len(blocks) * blocks[0][0].shape[2] ** 2
    spare = [jnp.zeros((width - 2 * half, cells), bf16)] if width > 2 * half else []
    acc[...] = jnp.zeros_like(acc)
    slot_id = lax.broadcasted_iota(jnp.int32, (slots, CHUNK), 0).astype(f32).astype(bf16)

    def one_row(r, carry):
        members, high, low = [], [], []
        for first in range(0, cells, CHUNK):
            cut = slice(first, first + CHUNK)
            here = slot[pl.ds(r, 1), cut].astype(f32).astype(bf16)
            members.append(
                jnp.where(
                    jnp.broadcast_to(here, (slots, CHUNK)) == slot_id,
                    jnp.ones((slots, CHUNK), bf16),
                    jnp.zeros((slots, CHUNK), bf16),
                )
            )
            top, rest = [], []
            for left, bend in blocks:
                right = [bend[c, r, :, cut] for c in range(3)]
                modes = right[0].shape[0]
                for i in range(0, modes, 2):
                    pair = []
                    for k in (i, i + 1):
                        spread = [
                            jnp.broadcast_to(left[c, r, pl.ds(k, 1), cut], (modes, CHUNK))
                            for c in range(3)
                        ]
                        pair.append(spread[0] * right[0] + spread[1] * right[1] + spread[2] * right[2])
                    product = jnp.concatenate(pair, axis=0)
                    top.append(product.astype(bf16))
                    rest.append((product - top[-1].astype(f32)).astype(bf16))
            high.append(jnp.concatenate(top, axis=0))
            low.append(jnp.concatenate(rest, axis=0))
        products = jnp.concatenate(
            [jnp.concatenate(high, axis=1), jnp.concatenate(low, axis=1)] + spare, axis=0
        )
        acc[...] += lax.dot_general(
            products, jnp.concatenate(members, axis=1), (((1,), (1,)), ((), ())), preferred_element_type=f32
        )
        return carry

    lax.fori_loop(0, rows, one_row, 0, unroll=2)
    return jnp.transpose(acc[0:half, :] + acc[half : 2 * half, :])


def stage_own(
    body, edge, stiff_far_away, slot_far_away,
    bend, left, total, sums, stiff, slot,
    plain, cross, second, acc, arrived,
):
    stiff_copy = pltpu.make_async_copy(stiff_far_away, stiff, arrived.at[0])
    slot_copy = pltpu.make_async_copy(slot_far_away, slot, arrived.at[1])
    stiff_copy.start()
    slot_copy.start()
    stiff_copy.wait()
    slot_copy.wait()
    stencil((body, edge), stiff, (plain, cross, second), bend, left, total)
    sums[...] = pair_sums(slot, [(left, bend)], acc)


def stage_near(
    below, below_edge, above, above_edge, stiff, slot, bend, left,
    bend_above, left_above, total_above, sums,
    bend_below, plain, cross, second, acc,
):
    lines = (plain, cross, second)
    stencil((below, below_edge), stiff, lines, bend_below)
    stencil((above, above_edge), stiff, lines, bend_above, left_above, total_above)
    blocks = [(left, bend_above), (left, bend_below), (left_above, bend_below)]
    sums[...] = pair_sums(slot, blocks, acc)


def stage_far(
    below, below_edge, above, above_edge, stiff, slot, left, bend_above, left_above,
    total, total_above, own_sums, near_sums,
    message,
    bend_far_below, left_far_below, bend_far_above, total_far_below, total_far_above,
    plain, cross, second, acc,
):
    lines = (plain, cross, second)
    stencil((below, below_edge), stiff, lines, bend_far_below, left_far_below, total_far_below)
    stencil((above, above_edge), stiff, lines, bend_far_above, None, total_far_above)
    blocks = [
        (left_above, bend_far_below), (left, bend_far_above),
        (left_far_below, bend_above), (left_far_below, bend_far_above),
    ]
    sums = pair_sums(slot, blocks, acc)
    owners, entries, _ = message.shape
    early = jnp.concatenate([near_sums[...], own_sums[...]], axis=1)
    message[:, :, 0:256] = early.reshape(owners, entries, 256)
    message[:, :, 256:512] = sums.reshape(owners, entries, 256)
    lane = lax.broadcasted_iota(jnp.int32, total.shape, 1)
    places = jnp.zeros(total.shape, f32)
    for place, panel in enumerate([total, total_above, total_far_above, total_far_below]):
        places = jnp.where(lane == place, panel[...], places)
    message[:, :, 512:640] = jnp.broadcast_to(places[None], (owners, entries, 128))


def three_parts(x):
    a = x.astype(bf16)
    rest = x - a.astype(f32)
    b = rest.astype(bf16)
    return a, b, (rest - b.astype(f32)).astype(bf16)


def exact_dot(x, y, parts_of_y):
    if parts_of_y:
        return sum(jnp.dot(x, part, preferred_element_type=f32) for part in three_parts(y))
    return sum(jnp.dot(part, y, preferred_element_type=f32) for part in three_parts(x))


def gather_zones(received, lists, mine, to_far, to_next):
    places, width = received.shape
    zones = mine.shape[0]
    body = width - 128
    chosen = jnp.broadcast_to(lists[...], (zones, places)) == lax.broadcasted_iota(
        jnp.int32, (zones, places), 0
    )
    chosen = jnp.where(chosen, 1.0, 0.0).astype(bf16)
    zoned = exact_dot(chosen, received[:, 0:body], True)
    totals = jnp.sum(received[:, body:].reshape(places // 8, 8, 128), axis=0)
    mine[...] = zoned[:, 0:128]
    to_far[0:8, :] = totals
    to_far[8:, :] = zoned[:, 384:512]
    to_next[0:8, :] = totals
    to_next[8 : zones + 8, :] = zoned[:, 128:256]
    to_next[zones + 8 :, :] = zoned[:, 256:384]


def normalise(place, mine, kept, from_far, from_below, energy):
    zones = energy.shape[0]
    t = slice(0, 8)
    y = slice(8, zones + 8)
    z = slice(zones + 8, 2 * zones + 8)
    sums = jnp.concatenate(
        [
            kept[y, 64:128], mine[:, 0:64], kept[z, 64:128], from_far[y, 0:64],
            from_far[y, 64:128], from_below[z, 0:64], from_below[y, 0:64], mine[:, 64:128],
        ],
        axis=1,
    )
    own, far, below = kept[t, :], from_far[t, :], from_below[t, :]
    columns = [
        own[:, 0:1], own[:, 1:2], own[:, 2:3], far[:, 1:2],
        far[:, 2:3], below[:, 3:4], own[:, 3:4], below[:, 0:1],
    ]
    spread = jnp.concatenate([jnp.broadcast_to(c, (8, 64)) for c in columns], axis=1)
    sub = lax.broadcasted_iota(jnp.int32, (8, 512), 0)
    lane = lax.broadcasted_iota(jnp.int32, (8, 512), 1)
    total_j = jnp.sum(jnp.where(lane % 8 == sub, spread, 0.0), axis=0, keepdims=True)
    total_i = jnp.sum(
        jnp.where((lane // 8) % 8 == sub, jnp.broadcast_to(own[:, 0:1], (8, 512)), 0.0), axis=0, keepdims=True
    )
    scaled = ZONES * (0.5 * sums) / jnp.sqrt((0.5 * total_i) * (0.5 * total_j))
    r = lax.broadcasted_iota(jnp.int32, (512, 512), 0)
    c = lax.broadcasted_iota(jnp.int32, (512, 512), 1)
    panel = (r // 64 + place[0]) % 8
    target = ((r // 8) % 8) * 64 + panel * 8 + r % 8
    order = jnp.where(c == target, 1.0, 0.0).astype(bf16)
    ordered = exact_dot(scaled, order, False)
    for i in range(8):
        energy[:, i, :] = ordered[:, i * 64 : (i + 1) * 64]


def vmem(shape, dtype=f32):
    return pltpu.VMEM(shape, dtype)


def call(body, outs, scratch, *args, spaces=()):
    where = list(spaces) + [pltpu.VMEM] * (len(args) - len(spaces))
    return pl.pallas_call(
        body,
        out_shape=[jax.ShapeDtypeStruct(s, d) for s, d in outs],
        in_specs=[pl.BlockSpec(memory_space=space) for space in where],
        out_specs=[pl.BlockSpec(memory_space=pltpu.VMEM)] * len(outs),
        scratch_shapes=scratch,
        compiler_params=pltpu.CompilerParams(vmem_limit_bytes=24 << 20),
    )(*args)


def per_device(mode_shapes, stiffness, node_slot, slot_zone):
    modes, rows, cells = mode_shapes.shape
    tiles = lax.axis_size("tile")
    panels = lax.axis_size("mode")
    entries = slot_zone.shape[2]
    slots = tiles * entries
    owned = ZONES // tiles
    up = [(i, i + 1) for i in range(tiles - 1)]
    down = [(i + 1, i) for i in range(tiles - 1)]

    def turn(x, by):
        return lax.ppermute(x, "mode", [(i, (i + by) % panels) for i in range(panels)])

    lists = lax.dynamic_index_in_dim(slot_zone, lax.axis_index("tile"), 1, keepdims=False)
    lists = lists.reshape(1, slots)
    head = lax.ppermute(mode_shapes[:, rows - 1], "tile", up)
    tail = lax.ppermute(mode_shapes[:, 0], "tile", down)
    inner = jnp.transpose(mode_shapes, (1, 0, 2))
    below = turn(inner, 1)
    above = turn(inner, -1)
    edge, lists = lax.optimization_barrier((jnp.stack([head, tail]), lists))
    below_edge = turn(edge, 1)
    above_edge = turn(edge, -1)
    far_below = turn(below, 1)
    far_above = turn(above, -1)
    far_below_edge = turn(below_edge, 1)
    far_above_edge = turn(above_edge, -1)

    factor = ((3, rows, modes, cells), f32)
    total = ((modes, 128), f32)
    lines = [vmem((rows + 2, modes, cells))] * 3
    pairs = modes * modes
    bend0, left0, total0, own_sums, stiff, slot = call(
        stage_own,
        [
            factor, factor, total, ((slots, pairs), f32),
            (stiffness.shape, stiffness.dtype), (node_slot.shape, node_slot.dtype),
        ],
        lines + [vmem((2 * pairs, slots)), pltpu.SemaphoreType.DMA((2,))],
        inner, edge, stiffness, node_slot,
        spaces=(pltpu.VMEM, pltpu.VMEM, pltpu.HBM, pltpu.HBM),
    )
    bend_above, left_above, total_above, near_sums = call(
        stage_near, [factor, factor, total, ((slots, 3 * pairs), f32)],
        [vmem(*factor)] + lines + [vmem((6 * pairs, slots))],
        below, below_edge, above, above_edge, stiff, slot, bend0, left0,
    )
    (message,) = call(
        stage_far, [((tiles, entries, 8 * pairs + 128), f32)],
        [vmem(*factor)] * 3 + [vmem(*total)] * 2 + lines + [vmem((8 * pairs, slots))],
        far_below, far_below_edge, far_above, far_above_edge, stiff, slot, left0, bend_above, left_above,
        total0, total_above, own_sums, near_sums,
    )
    message, lists = lax.optimization_barrier((message, lists))
    received = lax.all_to_all(message, "tile", 0, 0, tiled=True)
    mine, to_far, to_next = call(
        gather_zones,
        [((owned, 128), f32), ((owned + 8, 128), f32), ((2 * owned + 8, 128), f32)], [],
        received.reshape(slots, 8 * pairs + 128), lists,
    )
    from_far = turn(to_far, -2)
    from_below = turn(to_next, 1)
    place = lax.axis_index("mode").astype(jnp.int32).reshape(1)
    (energy,) = call(
        normalise, [((owned, modes, panels * modes), f32)], [],
        place, mine, to_next, from_far, from_below, spaces=(pltpu.SMEM,),
    )
    return energy


def solution(mesh):
    placed = (P("mode", "tile", None), P("tile", None), P("tile", None), P())

    return jax.shard_map(per_device, mesh=mesh, in_specs=placed, out_specs=P("tile", "mode", None), check_vma=False)
```

```python
import jax
import jax.numpy as jnp
from jax import lax
from jax.experimental import pallas as pl
from jax.experimental.pallas import tpu as pltpu
from jax.sharding import PartitionSpec as P


ZONES = 512
POISSON = 0.3
SHEAR = 2.0 * (1.0 - POISSON)
CHUNK = 512

f32 = jnp.float32
bf16 = jnp.bfloat16


def stencil(shapes, plate, lines, bend_out, left_out=None, total_out=None):
    framed_rows, modes, cells = shapes.shape
    plain, cross, second = lines
    lane = lax.broadcasted_iota(jnp.int32, (modes, cells), 1)
    group = 5

    def across(n, carry):
        for k in range(group):
            r = n * group + k
            w = shapes[r].astype(f32)
            right = jnp.where(lane == cells - 1, 0.0, pltpu.roll(w, cells - 1, 1))
            left = jnp.where(lane == 0, 0.0, pltpu.roll(w, 1, 1))
            plain[r] = w
            cross[r] = right - left
            second[r] = (right - 2.0 * w) + left
        return carry

    lax.fori_loop(0, framed_rows // group, across, 0)

    def along(r, total):
        along_x = (plain[r + 2] - 2.0 * plain[r + 1]) + plain[r]
        bent = [along_x, second[r + 1], 0.25 * (cross[r + 2] - cross[r])]
        bx, by, bt = [b.astype(bf16).astype(f32) for b in bent]
        for c, b in enumerate((bx, by, bt)):
            bend_out[c, r] = b
        if left_out is None and total_out is None:
            return total
        s = jnp.broadcast_to(plate[0, pl.ds(r, 1), :], (modes, cells))
        weighted = [s * (bx + POISSON * by), s * (by + POISSON * bx), s * (SHEAR * bt)]
        if left_out is not None:
            for c in range(3):
                left_out[c, r] = weighted[c].astype(bf16).astype(f32)
        if total_out is None:
            return total
        energy = weighted[0] * bx + weighted[1] * by + weighted[2] * bt
        for k in range(cells // 128):
            total = total + energy[:, k * 128 : (k + 1) * 128]
        return total

    total = lax.fori_loop(0, framed_rows - 2, along, jnp.zeros((modes, 128), f32))
    if total_out is not None:
        total_out[...] = jnp.broadcast_to(jnp.sum(total, axis=1, keepdims=True), (modes, 128))


def pair_sums(plate, blocks, acc):
    _, rows, cells = plate.shape
    width, slots = acc.shape
    half = len(blocks) * blocks[0][0].shape[2] ** 2
    spare = [jnp.zeros((width - 2 * half, cells), bf16)] if width > 2 * half else []
    acc[...] = jnp.zeros_like(acc)
    slot_id = lax.broadcasted_iota(jnp.int32, (slots, CHUNK), 0).astype(f32).astype(bf16)

    def one_row(r, carry):
        members, high, low = [], [], []
        for first in range(0, cells, CHUNK):
            cut = slice(first, first + CHUNK)
            here = plate[1, pl.ds(r, 1), cut].astype(bf16)
            members.append(
                jnp.where(
                    jnp.broadcast_to(here, (slots, CHUNK)) == slot_id,
                    jnp.ones((slots, CHUNK), bf16),
                    jnp.zeros((slots, CHUNK), bf16),
                )
            )
            top, rest = [], []
            for left, bend in blocks:
                right = [bend[c, r, :, cut] for c in range(3)]
                modes = right[0].shape[0]
                for i in range(0, modes, 2):
                    pair = []
                    for k in (i, i + 1):
                        spread = [
                            jnp.broadcast_to(left[c, r, pl.ds(k, 1), cut], (modes, CHUNK))
                            for c in range(3)
                        ]
                        pair.append(spread[0] * right[0] + spread[1] * right[1] + spread[2] * right[2])
                    product = jnp.concatenate(pair, axis=0)
                    top.append(product.astype(bf16))
                    rest.append((product - top[-1].astype(f32)).astype(bf16))
            high.append(jnp.concatenate(top, axis=0))
            low.append(jnp.concatenate(rest, axis=0))
        products = jnp.concatenate(
            [jnp.concatenate(high, axis=1), jnp.concatenate(low, axis=1)] + spare, axis=0
        )
        acc[...] += lax.dot_general(
            products, jnp.concatenate(members, axis=1), (((1,), (1,)), ((), ())), preferred_element_type=f32
        )
        return carry

    lax.fori_loop(0, rows, one_row, 0, unroll=2)
    return jnp.transpose(acc[0:half, :] + acc[half : 2 * half, :])


def stage_own(shapes, plate, bend, left, total, sums, plain, cross, second, acc):
    stencil(shapes, plate, (plain, cross, second), bend, left, total)
    sums[...] = pair_sums(plate, [(left, bend)], acc)


def stage_near(
    below, above, plate, bend, left,
    bend_above, left_above, total_above, sums,
    bend_below, plain, cross, second, acc,
):
    lines = (plain, cross, second)
    stencil(below, plate, lines, bend_below)
    stencil(above, plate, lines, bend_above, left_above, total_above)
    blocks = [(left, bend_above), (left, bend_below), (left_above, bend_below)]
    sums[...] = pair_sums(plate, blocks, acc)


def stage_far(
    below, above, plate, left, bend_above, left_above,
    total, total_above, own_sums, near_sums,
    message,
    bend_far_below, left_far_below, bend_far_above, total_far_below, total_far_above,
    plain, cross, second, acc,
):
    lines = (plain, cross, second)
    stencil(below, plate, lines, bend_far_below, left_far_below, total_far_below)
    stencil(above, plate, lines, bend_far_above, None, total_far_above)
    blocks = [
        (left_above, bend_far_below), (left, bend_far_above),
        (left_far_below, bend_above), (left_far_below, bend_far_above),
    ]
    sums = pair_sums(plate, blocks, acc)
    owners, entries, _ = message.shape
    early = jnp.concatenate([near_sums[...], own_sums[...]], axis=1)
    message[:, :, 0:256] = early.reshape(owners, entries, 256)
    message[:, :, 256:512] = sums.reshape(owners, entries, 256)
    lane = lax.broadcasted_iota(jnp.int32, total.shape, 1)
    places = jnp.zeros(total.shape, f32)
    for place, panel in enumerate([total, total_above, total_far_above, total_far_below]):
        places = jnp.where(lane == place, panel[...], places)
    message[:, :, 512:640] = jnp.broadcast_to(places[None], (owners, entries, 128))


def three_parts(x):
    a = x.astype(bf16)
    rest = x - a.astype(f32)
    b = rest.astype(bf16)
    return a, b, (rest - b.astype(f32)).astype(bf16)


def exact_dot(x, y, parts_of_y):
    if parts_of_y:
        return sum(jnp.dot(x, part, preferred_element_type=f32) for part in three_parts(y))
    return sum(jnp.dot(part, y, preferred_element_type=f32) for part in three_parts(x))


def gather_zones(received, lists, mine, to_far, to_next):
    places, width = received.shape
    zones = mine.shape[0]
    body = width - 128
    chosen = jnp.broadcast_to(lists[...], (zones, places)) == lax.broadcasted_iota(
        jnp.int32, (zones, places), 0
    )
    chosen = jnp.where(chosen, 1.0, 0.0).astype(bf16)
    zoned = exact_dot(chosen, received[:, 0:body], True)
    totals = jnp.sum(received[:, body:].reshape(places // 8, 8, 128), axis=0)
    mine[...] = zoned[:, 0:128]
    to_far[0:8, :] = totals
    to_far[8:, :] = zoned[:, 384:512]
    to_next[0:8, :] = totals
    to_next[8 : zones + 8, :] = zoned[:, 128:256]
    to_next[zones + 8 :, :] = zoned[:, 256:384]


def normalise(place, mine, kept, from_far, from_below, energy):
    zones = energy.shape[0]
    t = slice(0, 8)
    y = slice(8, zones + 8)
    z = slice(zones + 8, 2 * zones + 8)
    sums = jnp.concatenate(
        [
            kept[y, 64:128], mine[:, 0:64], kept[z, 64:128], from_far[y, 0:64],
            from_far[y, 64:128], from_below[z, 0:64], from_below[y, 0:64], mine[:, 64:128],
        ],
        axis=1,
    )
    own, far, below = kept[t, :], from_far[t, :], from_below[t, :]
    columns = [
        own[:, 0:1], own[:, 1:2], own[:, 2:3], far[:, 1:2],
        far[:, 2:3], below[:, 3:4], own[:, 3:4], below[:, 0:1],
    ]
    spread = jnp.concatenate([jnp.broadcast_to(c, (8, 64)) for c in columns], axis=1)
    sub = lax.broadcasted_iota(jnp.int32, (8, 512), 0)
    lane = lax.broadcasted_iota(jnp.int32, (8, 512), 1)
    total_j = jnp.sum(jnp.where(lane % 8 == sub, spread, 0.0), axis=0, keepdims=True)
    total_i = jnp.sum(
        jnp.where((lane // 8) % 8 == sub, jnp.broadcast_to(own[:, 0:1], (8, 512)), 0.0), axis=0, keepdims=True
    )
    scaled = ZONES * (0.5 * sums) / jnp.sqrt((0.5 * total_i) * (0.5 * total_j))
    r = lax.broadcasted_iota(jnp.int32, (512, 128), 0)
    c = lax.broadcasted_iota(jnp.int32, (512, 128), 1)
    target = ((r & 56) << 3) + ((((r >> 6) + place[0]) & 7) << 3) + (r & 7) - c
    order = jnp.concatenate(
        [jnp.where(target == first, 1.0, 0.0).astype(bf16) for first in range(0, 512, 128)], axis=1
    )
    ordered = exact_dot(scaled, order, False)
    for i in range(8):
        energy[:, i, :] = ordered[:, i * 64 : (i + 1) * 64]


def vmem(shape, dtype=f32):
    return pltpu.VMEM(shape, dtype)


def call(body, outs, scratch, *args, spaces=()):
    where = list(spaces) + [pltpu.VMEM] * (len(args) - len(spaces))
    return pl.pallas_call(
        body,
        out_shape=[jax.ShapeDtypeStruct(s, d) for s, d in outs],
        in_specs=[pl.BlockSpec(memory_space=space) for space in where],
        out_specs=[pl.BlockSpec(memory_space=pltpu.VMEM)] * len(outs),
        scratch_shapes=scratch,
        compiler_params=pltpu.CompilerParams(vmem_limit_bytes=24 << 20),
    )(*args)


def per_device(mode_shapes, stiffness, node_slot, slot_zone):
    modes, rows, cells = mode_shapes.shape
    tiles = lax.axis_size("tile")
    panels = lax.axis_size("mode")
    entries = slot_zone.shape[2]
    slots = tiles * entries
    owned = ZONES // tiles
    up = [(i, i + 1) for i in range(tiles - 1)]
    down = [(i + 1, i) for i in range(tiles - 1)]

    def turn(x, by):
        return lax.ppermute(x, "mode", [(i, (i + by) % panels) for i in range(panels)])

    lists = lax.dynamic_index_in_dim(slot_zone, lax.axis_index("tile"), 1, keepdims=False)
    lists = lists.reshape(1, slots)
    plate = jnp.stack([stiffness, node_slot.astype(f32)])
    head = lax.ppermute(mode_shapes[:, rows - 1], "tile", up)
    tail = lax.ppermute(mode_shapes[:, 0], "tile", down)
    framed = jnp.concatenate([head[None], jnp.transpose(mode_shapes, (1, 0, 2)), tail[None]], axis=0)
    framed, lists, plate = lax.optimization_barrier((framed, lists, plate))
    below = turn(framed, 1)
    above = turn(framed, -1)
    far_below = turn(below, 1)
    far_above = turn(above, -1)

    factor = ((3, rows, modes, cells), f32)
    total = ((modes, 128), f32)
    lines = [vmem((rows + 2, modes, cells))] * 3
    pairs = modes * modes
    bend0, left0, total0, own_sums = call(
        stage_own, [factor, factor, total, ((slots, pairs), f32)],
        lines + [vmem((2 * pairs, slots))],
        framed, plate,
    )
    bend_above, left_above, total_above, near_sums = call(
        stage_near, [factor, factor, total, ((slots, 3 * pairs), f32)],
        [vmem(*factor)] + lines + [vmem((6 * pairs, slots))],
        below, above, plate, bend0, left0,
    )
    (message,) = call(
        stage_far, [((tiles, entries, 8 * pairs + 128), f32)],
        [vmem(*factor)] * 3 + [vmem(*total)] * 2 + lines + [vmem((8 * pairs, slots))],
        far_below, far_above, plate, left0, bend_above, left_above,
        total0, total_above, own_sums, near_sums,
    )
    message, lists = lax.optimization_barrier((message, lists))
    received = lax.all_to_all(message, "tile", 0, 0, tiled=True)
    mine, to_far, to_next = call(
        gather_zones,
        [((owned, 128), f32), ((owned + 8, 128), f32), ((2 * owned + 8, 128), f32)], [],
        received.reshape(slots, 8 * pairs + 128), lists,
    )
    from_far = turn(to_far, -2)
    from_below = turn(to_next, 1)
    place = lax.axis_index("mode").astype(jnp.int32).reshape(1)
    (energy,) = call(
        normalise, [((owned, modes, panels * modes), f32)], [],
        place, mine, to_next, from_far, from_below, spaces=(pltpu.SMEM,),
    )
    return energy


def solution(mesh):
    placed = (P("mode", "tile", None), P("tile", None), P("tile", None), P())

    return jax.shard_map(per_device, mesh=mesh, in_specs=placed, out_specs=P("tile", "mode", None), check_vma=False)
```

```python
import jax
import jax.numpy as jnp
from jax import lax
from jax.experimental import pallas as pl
from jax.experimental.pallas import tpu as pltpu
from jax.sharding import PartitionSpec as P


ZONES = 512
POISSON = 0.3
SHEAR = 2.0 * (1.0 - POISSON)
CHUNK = 512

f32 = jnp.float32
bf16 = jnp.bfloat16


def stencil(shapes, plate, lines, bend_out, left_out=None, total_out=None):
    framed_rows, modes, cells = shapes.shape
    plain, cross, second = lines
    lane = lax.broadcasted_iota(jnp.int32, (modes, cells), 1)
    group = 5

    def across(n, carry):
        for k in range(group):
            r = n * group + k
            w = shapes[r].astype(f32)
            right = jnp.where(lane == cells - 1, 0.0, pltpu.roll(w, cells - 1, 1))
            left = jnp.where(lane == 0, 0.0, pltpu.roll(w, 1, 1))
            plain[r] = w
            cross[r] = right - left
            second[r] = (right - 2.0 * w) + left
        return carry

    lax.fori_loop(0, framed_rows // group, across, 0)

    def along(r, total):
        along_x = (plain[r + 2] - 2.0 * plain[r + 1]) + plain[r]
        bent = [along_x, second[r + 1], 0.25 * (cross[r + 2] - cross[r])]
        bx, by, bt = [b.astype(bf16).astype(f32) for b in bent]
        for c, b in enumerate((bx, by, bt)):
            bend_out[c, r] = b
        if left_out is None and total_out is None:
            return total
        s = jnp.broadcast_to(plate[0, pl.ds(r, 1), :], (modes, cells))
        weighted = [s * (bx + POISSON * by), s * (by + POISSON * bx), s * (SHEAR * bt)]
        if left_out is not None:
            for c in range(3):
                left_out[c, r] = weighted[c].astype(bf16).astype(f32)
        if total_out is None:
            return total
        energy = weighted[0] * bx + weighted[1] * by + weighted[2] * bt
        for k in range(cells // 128):
            total = total + energy[:, k * 128 : (k + 1) * 128]
        return total

    total = lax.fori_loop(0, framed_rows - 2, along, jnp.zeros((modes, 128), f32))
    if total_out is not None:
        total_out[...] = jnp.broadcast_to(jnp.sum(total, axis=1, keepdims=True), (modes, 128))


def pair_sums(plate, blocks, acc):
    _, rows, cells = plate.shape
    width, slots = acc.shape
    half = len(blocks) * blocks[0][0].shape[2] ** 2
    spare = [jnp.zeros((width - 2 * half, cells), bf16)] if width > 2 * half else []
    acc[...] = jnp.zeros_like(acc)
    slot_id = lax.broadcasted_iota(jnp.int32, (slots, CHUNK), 0).astype(f32).astype(bf16)

    def one_row(r, carry):
        members, high, low = [], [], []
        for first in range(0, cells, CHUNK):
            cut = slice(first, first + CHUNK)
            here = plate[1, pl.ds(r, 1), cut].astype(bf16)
            members.append(
                jnp.where(
                    jnp.broadcast_to(here, (slots, CHUNK)) == slot_id,
                    jnp.ones((slots, CHUNK), bf16),
                    jnp.zeros((slots, CHUNK), bf16),
                )
            )
            top, rest = [], []
            for left, bend in blocks:
                right = [bend[c, r, :, cut] for c in range(3)]
                modes = right[0].shape[0]
                for i in range(0, modes, 2):
                    pair = []
                    for k in (i, i + 1):
                        spread = [
                            jnp.broadcast_to(left[c, r, pl.ds(k, 1), cut], (modes, CHUNK))
                            for c in range(3)
                        ]
                        pair.append(spread[0] * right[0] + spread[1] * right[1] + spread[2] * right[2])
                    product = jnp.concatenate(pair, axis=0)
                    top.append(product.astype(bf16))
                    rest.append((product - top[-1].astype(f32)).astype(bf16))
            high.append(jnp.concatenate(top, axis=0))
            low.append(jnp.concatenate(rest, axis=0))
        products = jnp.concatenate(
            [jnp.concatenate(high, axis=1), jnp.concatenate(low, axis=1)] + spare, axis=0
        )
        acc[...] += lax.dot_general(
            products, jnp.concatenate(members, axis=1), (((1,), (1,)), ((), ())), preferred_element_type=f32
        )
        return carry

    lax.fori_loop(0, rows, one_row, 0, unroll=2)
    return jnp.transpose(acc[0:half, :] + acc[half : 2 * half, :])


def stage_own(place, shapes, plate, bend, left, total, sums, order, plain, cross, second, acc):
    stencil(shapes, plate, (plain, cross, second), bend, left, total)
    size = order.shape[0]
    r = lax.broadcasted_iota(jnp.int32, (size, 128), 0)
    c = lax.broadcasted_iota(jnp.int32, (size, 128), 1)
    target = ((r & 56) << 3) + ((((r >> 6) + place[0]) & 7) << 3) + (r & 7) - c
    for first in range(0, size, 128):
        order[:, first : first + 128] = jnp.where(target == first, 1.0, 0.0).astype(bf16)
    sums[...] = pair_sums(plate, [(left, bend)], acc)


def stage_near(
    below, above, plate, bend, left,
    bend_above, left_above, total_above, sums,
    bend_below, plain, cross, second, acc,
):
    lines = (plain, cross, second)
    stencil(below, plate, lines, bend_below)
    stencil(above, plate, lines, bend_above, left_above, total_above)
    blocks = [(left, bend_above), (left, bend_below), (left_above, bend_below)]
    sums[...] = pair_sums(plate, blocks, acc)


def stage_far(
    below, above, plate, left, bend_above, left_above,
    total, total_above, own_sums, near_sums,
    message,
    bend_far_below, left_far_below, bend_far_above, total_far_below, total_far_above,
    plain, cross, second, acc,
):
    lines = (plain, cross, second)
    stencil(below, plate, lines, bend_far_below, left_far_below, total_far_below)
    stencil(above, plate, lines, bend_far_above, None, total_far_above)
    blocks = [
        (left_above, bend_far_below), (left, bend_far_above),
        (left_far_below, bend_above), (left_far_below, bend_far_above),
    ]
    sums = pair_sums(plate, blocks, acc)
    owners, entries, _ = message.shape
    early = jnp.concatenate([near_sums[...], own_sums[...]], axis=1)
    message[:, :, 0:256] = early.reshape(owners, entries, 256)
    message[:, :, 256:512] = sums.reshape(owners, entries, 256)
    lane = lax.broadcasted_iota(jnp.int32, total.shape, 1)
    places = jnp.zeros(total.shape, f32)
    for place, panel in enumerate([total, total_above, total_far_above, total_far_below]):
        places = jnp.where(lane == place, panel[...], places)
    message[:, :, 512:640] = jnp.broadcast_to(places[None], (owners, entries, 128))


def three_parts(x):
    a = x.astype(bf16)
    rest = x - a.astype(f32)
    b = rest.astype(bf16)
    return a, b, (rest - b.astype(f32)).astype(bf16)


def gather_zones(received, lists, mine, to_far, to_next):
    places, width = received.shape
    zones = mine.shape[0]
    body = width - 128
    chosen = jnp.broadcast_to(lists[...], (zones, places)) == lax.broadcasted_iota(
        jnp.int32, (zones, places), 0
    )
    chosen = jnp.where(chosen, 1.0, 0.0).astype(bf16)
    zoned = sum(
        jnp.dot(chosen, part, preferred_element_type=f32) for part in three_parts(received[:, 0:body])
    )
    totals = jnp.sum(received[:, body:].reshape(places // 8, 8, 128), axis=0)
    mine[...] = zoned[:, 0:128]
    to_far[0:8, :] = totals
    to_far[8:, :] = zoned[:, 384:512]
    to_next[0:8, :] = totals
    to_next[8 : zones + 8, :] = zoned[:, 128:256]
    to_next[zones + 8 :, :] = zoned[:, 256:384]


def normalise(order, mine, kept, from_far, from_below, energy):
    zones = energy.shape[0]
    t = slice(0, 8)
    y = slice(8, zones + 8)
    z = slice(zones + 8, 2 * zones + 8)
    sums = jnp.concatenate(
        [
            kept[y, 64:128], mine[:, 0:64], kept[z, 64:128], from_far[y, 0:64],
            from_far[y, 64:128], from_below[z, 0:64], from_below[y, 0:64], mine[:, 64:128],
        ],
        axis=1,
    )
    own, far, below = kept[t, :], from_far[t, :], from_below[t, :]
    columns = [
        own[:, 0:1], own[:, 1:2], own[:, 2:3], far[:, 1:2],
        far[:, 2:3], below[:, 3:4], own[:, 3:4], below[:, 0:1],
    ]
    spread = jnp.concatenate([jnp.broadcast_to(c, (8, 64)) for c in columns], axis=1)
    sub = lax.broadcasted_iota(jnp.int32, (8, 512), 0)
    lane = lax.broadcasted_iota(jnp.int32, (8, 512), 1)
    total_j = jnp.sum(jnp.where((lane & 7) == sub, spread, 0.0), axis=0, keepdims=True)
    total_i = jnp.sum(
        jnp.where(((lane >> 3) & 7) == sub, jnp.broadcast_to(own[:, 0:1], (8, 512)), 0.0), axis=0, keepdims=True
    )
    scaled = ZONES * (0.5 * sums) / jnp.sqrt((0.5 * total_i) * (0.5 * total_j))
    parts = jnp.dot(jnp.concatenate(three_parts(scaled), axis=0), order[...], preferred_element_type=f32)
    ordered = parts[0:zones] + parts[zones : 2 * zones] + parts[2 * zones :]
    for i in range(8):
        energy[:, i, :] = ordered[:, i * 64 : (i + 1) * 64]


def vmem(shape, dtype=f32):
    return pltpu.VMEM(shape, dtype)


def call(body, outs, scratch, *args, spaces=()):
    where = list(spaces) + [pltpu.VMEM] * (len(args) - len(spaces))
    return pl.pallas_call(
        body,
        out_shape=[jax.ShapeDtypeStruct(s, d) for s, d in outs],
        in_specs=[pl.BlockSpec(memory_space=space) for space in where],
        out_specs=[pl.BlockSpec(memory_space=pltpu.VMEM)] * len(outs),
        scratch_shapes=scratch,
        compiler_params=pltpu.CompilerParams(vmem_limit_bytes=24 << 20),
    )(*args)


def per_device(mode_shapes, stiffness, node_slot, slot_zone):
    modes, rows, cells = mode_shapes.shape
    tiles = lax.axis_size("tile")
    panels = lax.axis_size("mode")
    entries = slot_zone.shape[2]
    slots = tiles * entries
    owned = ZONES // tiles
    up = [(i, i + 1) for i in range(tiles - 1)]
    down = [(i + 1, i) for i in range(tiles - 1)]

    def turn(x, by):
        return lax.ppermute(x, "mode", [(i, (i + by) % panels) for i in range(panels)])

    lists = lax.dynamic_index_in_dim(slot_zone, lax.axis_index("tile"), 1, keepdims=False)
    lists = lists.reshape(1, slots)
    head = lax.ppermute(mode_shapes[:, rows - 1], "tile", up)
    tail = lax.ppermute(mode_shapes[:, 0], "tile", down)
    framed = jnp.concatenate([head[None], jnp.transpose(mode_shapes, (1, 0, 2)), tail[None]], axis=0)
    framed, lists, rigid, named = lax.optimization_barrier((framed, lists, stiffness, node_slot))
    plate = jnp.stack([rigid, named.astype(f32)])
    below = turn(framed, 1)
    above = turn(framed, -1)
    far_below = turn(below, 1)
    far_above = turn(above, -1)

    factor = ((3, rows, modes, cells), f32)
    total = ((modes, 128), f32)
    lines = [vmem((rows + 2, modes, cells))] * 3
    pairs = modes * modes
    place = lax.axis_index("mode").astype(jnp.int32).reshape(1)
    bend0, left0, total0, own_sums, order = call(
        stage_own, [factor, factor, total, ((slots, pairs), f32), ((8 * pairs, 8 * pairs), bf16)],
        lines + [vmem((2 * pairs, slots))],
        place, framed, plate, spaces=(pltpu.SMEM,),
    )
    bend_above, left_above, total_above, near_sums = call(
        stage_near, [factor, factor, total, ((slots, 3 * pairs), f32)],
        [vmem(*factor)] + lines + [vmem((6 * pairs, slots))],
        below, above, plate, bend0, left0,
    )
    (message,) = call(
        stage_far, [((tiles, entries, 8 * pairs + 128), f32)],
        [vmem(*factor)] * 3 + [vmem(*total)] * 2 + lines + [vmem((8 * pairs, slots))],
        far_below, far_above, plate, left0, bend_above, left_above,
        total0, total_above, own_sums, near_sums,
    )
    message, lists = lax.optimization_barrier((message, lists))
    received = lax.all_to_all(message, "tile", 0, 0, tiled=True)
    mine, to_far, to_next = call(
        gather_zones,
        [((owned, 128), f32), ((owned + 8, 128), f32), ((2 * owned + 8, 128), f32)], [],
        received.reshape(slots, 8 * pairs + 128), lists,
    )
    from_far = turn(to_far, -2)
    from_below = turn(to_next, 1)
    (energy,) = call(
        normalise, [((owned, modes, panels * modes), f32)], [],
        order, mine, to_next, from_far, from_below,
    )
    return energy


def solution(mesh):
    placed = (P("mode", "tile", None), P("tile", None), P("tile", None), P())

    return jax.shard_map(per_device, mesh=mesh, in_specs=placed, out_specs=P("tile", "mode", None), check_vma=False)
```

```python
import jax
import jax.numpy as jnp
from jax import lax
from jax.experimental import pallas as pl
from jax.experimental.pallas import tpu as pltpu
from jax.sharding import PartitionSpec as P


ZONES = 512
POISSON = 0.3
SHEAR = 2.0 * (1.0 - POISSON)
CHUNK = 512

f32 = jnp.float32
bf16 = jnp.bfloat16


def stencil(shapes, plate, lines, bend_out, left_out=None, total_out=None):
    framed_rows, modes, cells = shapes.shape
    plain, cross, second = lines
    lane = lax.broadcasted_iota(jnp.int32, (modes, cells), 1)
    group = 5

    def across(n, carry):
        for k in range(group):
            r = n * group + k
            w = shapes[r].astype(f32)
            right = jnp.where(lane == cells - 1, 0.0, pltpu.roll(w, cells - 1, 1))
            left = jnp.where(lane == 0, 0.0, pltpu.roll(w, 1, 1))
            plain[r] = w
            cross[r] = right - left
            second[r] = (right - 2.0 * w) + left
        return carry

    lax.fori_loop(0, framed_rows // group, across, 0)

    def along(r, total):
        along_x = (plain[r + 2] - 2.0 * plain[r + 1]) + plain[r]
        bent = [along_x, second[r + 1], 0.25 * (cross[r + 2] - cross[r])]
        bx, by, bt = [b.astype(bf16).astype(f32) for b in bent]
        for c, b in enumerate((bx, by, bt)):
            bend_out[c, r] = b
        if left_out is None and total_out is None:
            return total
        s = jnp.broadcast_to(plate[0, pl.ds(r, 1), :], (modes, cells))
        weighted = [s * (bx + POISSON * by), s * (by + POISSON * bx), s * (SHEAR * bt)]
        if left_out is not None:
            for c in range(3):
                left_out[c, r] = weighted[c].astype(bf16).astype(f32)
        if total_out is None:
            return total
        energy = weighted[0] * bx + weighted[1] * by + weighted[2] * bt
        for k in range(cells // 128):
            total = total + energy[:, k * 128 : (k + 1) * 128]
        return total

    total = lax.fori_loop(0, framed_rows - 2, along, jnp.zeros((modes, 128), f32))
    if total_out is not None:
        total_out[...] = jnp.broadcast_to(jnp.sum(total, axis=1, keepdims=True), (modes, 128))


def pair_sums(plate, blocks, acc):
    _, rows, cells = plate.shape
    width, slots = acc.shape
    half = len(blocks) * blocks[0][0].shape[2] ** 2
    spare = [jnp.zeros((width - 2 * half, cells), bf16)] if width > 2 * half else []
    acc[...] = jnp.zeros_like(acc)
    slot_id = lax.broadcasted_iota(jnp.int32, (slots, CHUNK), 0).astype(f32).astype(bf16)

    def one_row(r, carry):
        members, high, low = [], [], []
        for first in range(0, cells, CHUNK):
            cut = slice(first, first + CHUNK)
            here = plate[1, pl.ds(r, 1), cut].astype(bf16)
            members.append(
                jnp.where(
                    jnp.broadcast_to(here, (slots, CHUNK)) == slot_id,
                    jnp.ones((slots, CHUNK), bf16),
                    jnp.zeros((slots, CHUNK), bf16),
                )
            )
            top, rest = [], []
            for left, bend in blocks:
                right = [bend[c, r, :, cut] for c in range(3)]
                modes = right[0].shape[0]
                for i in range(0, modes, 2):
                    pair = []
                    for k in (i, i + 1):
                        spread = [
                            jnp.broadcast_to(left[c, r, pl.ds(k, 1), cut], (modes, CHUNK))
                            for c in range(3)
                        ]
                        pair.append(spread[0] * right[0] + spread[1] * right[1] + spread[2] * right[2])
                    product = jnp.concatenate(pair, axis=0)
                    top.append(product.astype(bf16))
                    rest.append((product - top[-1].astype(f32)).astype(bf16))
            high.append(jnp.concatenate(top, axis=0))
            low.append(jnp.concatenate(rest, axis=0))
        products = jnp.concatenate(
            [jnp.concatenate(high, axis=1), jnp.concatenate(low, axis=1)] + spare, axis=0
        )
        acc[...] += lax.dot_general(
            products, jnp.concatenate(members, axis=1), (((1,), (1,)), ((), ())), preferred_element_type=f32
        )
        return carry

    lax.fori_loop(0, rows, one_row, 0, unroll=4)
    return jnp.transpose(acc[0:half, :] + acc[half : 2 * half, :])


def stage_own(place, shapes, plate, bend, left, total, sums, order, plain, cross, second, acc):
    stencil(shapes, plate, (plain, cross, second), bend, left, total)
    size = order.shape[0]
    r = lax.broadcasted_iota(jnp.int32, (size, 128), 0)
    c = lax.broadcasted_iota(jnp.int32, (size, 128), 1)
    target = ((r & 56) << 3) + ((((r >> 6) + place[0]) & 7) << 3) + (r & 7) - c
    for first in range(0, size, 128):
        order[:, first : first + 128] = jnp.where(target == first, 1.0, 0.0).astype(bf16)
    sums[...] = pair_sums(plate, [(left, bend)], acc)


def stage_near(
    below, above, plate, bend, left,
    bend_above, left_above, total_above, sums,
    bend_below, plain, cross, second, acc,
):
    lines = (plain, cross, second)
    stencil(below, plate, lines, bend_below)
    stencil(above, plate, lines, bend_above, left_above, total_above)
    blocks = [(left, bend_above), (left, bend_below), (left_above, bend_below)]
    sums[...] = pair_sums(plate, blocks, acc)


def stage_far(
    below, above, plate, left, bend_above, left_above,
    total, total_above, own_sums, near_sums,
    message,
    bend_far_below, left_far_below, bend_far_above, total_far_below, total_far_above,
    plain, cross, second, acc,
):
    lines = (plain, cross, second)
    stencil(below, plate, lines, bend_far_below, left_far_below, total_far_below)
    stencil(above, plate, lines, bend_far_above, None, total_far_above)
    blocks = [
        (left_above, bend_far_below), (left, bend_far_above),
        (left_far_below, bend_above), (left_far_below, bend_far_above),
    ]
    sums = pair_sums(plate, blocks, acc)
    owners, entries, _ = message.shape
    early = jnp.concatenate([near_sums[...], own_sums[...]], axis=1)
    message[:, :, 0:256] = early.reshape(owners, entries, 256)
    message[:, :, 256:512] = sums.reshape(owners, entries, 256)
    lane = lax.broadcasted_iota(jnp.int32, total.shape, 1)
    places = jnp.zeros(total.shape, f32)
    for place, panel in enumerate([total, total_above, total_far_above, total_far_below]):
        places = jnp.where(lane == place, panel[...], places)
    message[:, :, 512:640] = jnp.broadcast_to(places[None], (owners, entries, 128))


def three_parts(x):
    a = x.astype(bf16)
    rest = x - a.astype(f32)
    b = rest.astype(bf16)
    return a, b, (rest - b.astype(f32)).astype(bf16)


def gather_zones(received, lists, mine, to_far, to_next):
    places, width = received.shape
    zones = mine.shape[0]
    body = width - 128
    chosen = jnp.broadcast_to(lists[...], (zones, places)) == lax.broadcasted_iota(
        jnp.int32, (zones, places), 0
    )
    chosen = jnp.where(chosen, 1.0, 0.0).astype(bf16)
    zoned = sum(
        jnp.dot(chosen, part, preferred_element_type=f32) for part in three_parts(received[:, 0:body])
    )
    totals = jnp.sum(received[:, body:].reshape(places // 8, 8, 128), axis=0)
    mine[...] = zoned[:, 0:128]
    to_far[0:8, :] = totals
    to_far[8:, :] = zoned[:, 384:512]
    to_next[0:8, :] = totals
    to_next[8 : zones + 8, :] = zoned[:, 128:256]
    to_next[zones + 8 :, :] = zoned[:, 256:384]


def normalise(order, mine, kept, from_far, from_below, energy):
    zones = energy.shape[0]
    t = slice(0, 8)
    y = slice(8, zones + 8)
    z = slice(zones + 8, 2 * zones + 8)
    sums = jnp.concatenate(
        [
            kept[y, 64:128], mine[:, 0:64], kept[z, 64:128], from_far[y, 0:64],
            from_far[y, 64:128], from_below[z, 0:64], from_below[y, 0:64], mine[:, 64:128],
        ],
        axis=1,
    )
    own, far, below = kept[t, :], from_far[t, :], from_below[t, :]
    columns = [
        own[:, 0:1], own[:, 1:2], own[:, 2:3], far[:, 1:2],
        far[:, 2:3], below[:, 3:4], own[:, 3:4], below[:, 0:1],
    ]
    spread = jnp.concatenate([jnp.broadcast_to(c, (8, 64)) for c in columns], axis=1)
    sub = lax.broadcasted_iota(jnp.int32, (8, 512), 0)
    lane = lax.broadcasted_iota(jnp.int32, (8, 512), 1)
    total_j = jnp.sum(jnp.where((lane & 7) == sub, spread, 0.0), axis=0, keepdims=True)
    total_i = jnp.sum(
        jnp.where(((lane >> 3) & 7) == sub, jnp.broadcast_to(own[:, 0:1], (8, 512)), 0.0), axis=0, keepdims=True
    )
    scaled = ZONES * (0.5 * sums) / jnp.sqrt((0.5 * total_i) * (0.5 * total_j))
    parts = jnp.dot(jnp.concatenate(three_parts(scaled), axis=0), order[...], preferred_element_type=f32)
    ordered = parts[0:zones] + parts[zones : 2 * zones] + parts[2 * zones :]
    for i in range(8):
        energy[:, i, :] = ordered[:, i * 64 : (i + 1) * 64]


def vmem(shape, dtype=f32):
    return pltpu.VMEM(shape, dtype)


def call(body, outs, scratch, *args, spaces=()):
    where = list(spaces) + [pltpu.VMEM] * (len(args) - len(spaces))
    return pl.pallas_call(
        body,
        out_shape=[jax.ShapeDtypeStruct(s, d) for s, d in outs],
        in_specs=[pl.BlockSpec(memory_space=space) for space in where],
        out_specs=[pl.BlockSpec(memory_space=pltpu.VMEM)] * len(outs),
        scratch_shapes=scratch,
        compiler_params=pltpu.CompilerParams(vmem_limit_bytes=24 << 20),
    )(*args)


def per_device(mode_shapes, stiffness, node_slot, slot_zone):
    modes, rows, cells = mode_shapes.shape
    tiles = lax.axis_size("tile")
    panels = lax.axis_size("mode")
    entries = slot_zone.shape[2]
    slots = tiles * entries
    owned = ZONES // tiles
    up = [(i, i + 1) for i in range(tiles - 1)]
    down = [(i + 1, i) for i in range(tiles - 1)]

    def turn(x, by):
        return lax.ppermute(x, "mode", [(i, (i + by) % panels) for i in range(panels)])

    row = lax.broadcasted_iota(jnp.int32, mode_shapes.shape, 1)
    last = jnp.sum(jnp.where(row == rows - 1, mode_shapes, 0), axis=1)
    first = jnp.sum(jnp.where(row == 0, mode_shapes, 0), axis=1)
    head = lax.ppermute(last, "tile", up)
    tail = lax.ppermute(first, "tile", down)
    framed = jnp.concatenate([head[None], jnp.transpose(mode_shapes, (1, 0, 2)), tail[None]], axis=0)
    framed, rigid, named, places = lax.optimization_barrier((framed, stiffness, node_slot, slot_zone))
    plate = jnp.stack([rigid, named.astype(f32)])
    lists = lax.dynamic_index_in_dim(places, lax.axis_index("tile"), 1, keepdims=False).reshape(1, slots)
    plate, lists = lax.optimization_barrier((plate, lists))
    below = turn(framed, 1)
    above = turn(framed, -1)
    far_below = turn(below, 1)
    far_above = turn(above, -1)

    factor = ((3, rows, modes, cells), f32)
    total = ((modes, 128), f32)
    lines = [vmem((rows + 2, modes, cells))] * 3
    pairs = modes * modes
    place = lax.axis_index("mode").astype(jnp.int32).reshape(1)
    bend0, left0, total0, own_sums, order = call(
        stage_own, [factor, factor, total, ((slots, pairs), f32), ((8 * pairs, 8 * pairs), bf16)],
        lines + [vmem((2 * pairs, slots))],
        place, framed, plate, spaces=(pltpu.SMEM,),
    )
    bend_above, left_above, total_above, near_sums = call(
        stage_near, [factor, factor, total, ((slots, 3 * pairs), f32)],
        [vmem(*factor)] + lines + [vmem((6 * pairs, slots))],
        below, above, plate, bend0, left0,
    )
    (message,) = call(
        stage_far, [((tiles, entries, 8 * pairs + 128), f32)],
        [vmem(*factor)] * 3 + [vmem(*total)] * 2 + lines + [vmem((8 * pairs, slots))],
        far_below, far_above, plate, left0, bend_above, left_above,
        total0, total_above, own_sums, near_sums,
    )
    message, lists = lax.optimization_barrier((message, lists))
    received = lax.all_to_all(message, "tile", 0, 0, tiled=True)
    mine, to_far, to_next = call(
        gather_zones,
        [((owned, 128), f32), ((owned + 8, 128), f32), ((2 * owned + 8, 128), f32)], [],
        received.reshape(slots, 8 * pairs + 128), lists,
    )
    from_far = turn(to_far, -2)
    from_below = turn(to_next, 1)
    (energy,) = call(
        normalise, [((owned, modes, panels * modes), f32)], [],
        order, mine, to_next, from_far, from_below,
    )
    return energy


def solution(mesh):
    placed = (P("mode", "tile", None), P("tile", None), P("tile", None), P())

    return jax.shard_map(per_device, mesh=mesh, in_specs=placed, out_specs=P("tile", "mode", None), check_vma=False)
```

```python
import jax
import jax.numpy as jnp
from jax import lax
from jax.experimental import pallas as pl
from jax.experimental.pallas import tpu as pltpu
from jax.sharding import PartitionSpec as P


ZONES = 512
POISSON = 0.3
SHEAR = 2.0 * (1.0 - POISSON)
CHUNK = 512

f32 = jnp.float32
bf16 = jnp.bfloat16


def stencil(shapes, plate, lines, bend_out, left_out=None, total_out=None):
    framed_rows, modes, cells = shapes.shape
    plain, cross, second = lines
    lane = lax.broadcasted_iota(jnp.int32, (modes, cells), 1)
    group = 5

    def across(n, carry):
        for k in range(group):
            r = n * group + k
            w = shapes[r].astype(f32)
            right = jnp.where(lane == cells - 1, 0.0, pltpu.roll(w, cells - 1, 1))
            left = jnp.where(lane == 0, 0.0, pltpu.roll(w, 1, 1))
            plain[r] = w
            cross[r] = right - left
            second[r] = (right - 2.0 * w) + left
        return carry

    lax.fori_loop(0, framed_rows // group, across, 0)

    def along(r, total):
        along_x = (plain[r + 2] - 2.0 * plain[r + 1]) + plain[r]
        bent = [along_x, second[r + 1], 0.25 * (cross[r + 2] - cross[r])]
        bx, by, bt = [b.astype(bf16).astype(f32) for b in bent]
        for c, b in enumerate((bx, by, bt)):
            bend_out[c, r] = b
        if left_out is None and total_out is None:
            return total
        s = jnp.broadcast_to(plate[0, pl.ds(r, 1), :], (modes, cells))
        weighted = [s * (bx + POISSON * by), s * (by + POISSON * bx), s * (SHEAR * bt)]
        if left_out is not None:
            for c in range(3):
                left_out[c, r] = weighted[c].astype(bf16).astype(f32)
        if total_out is None:
            return total
        energy = weighted[0] * bx + weighted[1] * by + weighted[2] * bt
        for k in range(cells // 128):
            total = total + energy[:, k * 128 : (k + 1) * 128]
        return total

    total = lax.fori_loop(0, framed_rows - 2, along, jnp.zeros((modes, 128), f32))
    if total_out is not None:
        total_out[...] = jnp.broadcast_to(jnp.sum(total, axis=1, keepdims=True), (modes, 128))


def pair_sums(plate, blocks, acc):
    _, rows, cells = plate.shape
    width, slots = acc.shape
    half = len(blocks) * blocks[0][0].shape[2] ** 2
    spare = [jnp.zeros((width - 2 * half, cells), bf16)] if width > 2 * half else []
    acc[...] = jnp.zeros_like(acc)
    slot_id = lax.broadcasted_iota(jnp.int32, (slots, CHUNK), 0).astype(f32).astype(bf16)

    def one_row(r, carry):
        members, high, low = [], [], []
        for first in range(0, cells, CHUNK):
            cut = slice(first, first + CHUNK)
            here = plate[1, pl.ds(r, 1), cut].astype(bf16)
            members.append(
                jnp.where(
                    jnp.broadcast_to(here, (slots, CHUNK)) == slot_id,
                    jnp.ones((slots, CHUNK), bf16),
                    jnp.zeros((slots, CHUNK), bf16),
                )
            )
            top, rest = [], []
            for left, bend in blocks:
                right = [bend[c, r, :, cut] for c in range(3)]
                modes = right[0].shape[0]
                for i in range(0, modes, 2):
                    pair = []
                    for k in (i, i + 1):
                        spread = [
                            jnp.broadcast_to(left[c, r, pl.ds(k, 1), cut], (modes, CHUNK))
                            for c in range(3)
                        ]
                        pair.append(spread[0] * right[0] + spread[1] * right[1] + spread[2] * right[2])
                    product = jnp.concatenate(pair, axis=0)
                    top.append(product.astype(bf16))
                    rest.append((product - top[-1].astype(f32)).astype(bf16))
            high.append(jnp.concatenate(top, axis=0))
            low.append(jnp.concatenate(rest, axis=0))
        products = jnp.concatenate(
            [jnp.concatenate(high, axis=1), jnp.concatenate(low, axis=1)] + spare, axis=0
        )
        acc[...] += lax.dot_general(
            products, jnp.concatenate(members, axis=1), (((1,), (1,)), ((), ())), preferred_element_type=f32
        )
        return carry

    lax.fori_loop(0, rows, one_row, 0, unroll=4)
    return jnp.transpose(acc[0:half, :] + acc[half : 2 * half, :])


def stage_own(place, shapes, plate, bend, left, total, sums, order, plain, cross, second, acc):
    stencil(shapes, plate, (plain, cross, second), bend, left, total)
    size = order.shape[0]
    r = lax.broadcasted_iota(jnp.int32, (size, 128), 0)
    c = lax.broadcasted_iota(jnp.int32, (size, 128), 1)
    target = ((r & 56) << 3) + ((((r >> 6) + place[0]) & 7) << 3) + (r & 7) - c
    for first in range(0, size, 128):
        order[:, first : first + 128] = jnp.where(target == first, 1.0, 0.0).astype(bf16)
    sums[...] = pair_sums(plate, [(left, bend)], acc)


def stage_near(
    below, above, plate, bend, left,
    bend_above, left_above, total_above, sums,
    bend_below, plain, cross, second, acc,
):
    lines = (plain, cross, second)
    stencil(below, plate, lines, bend_below)
    stencil(above, plate, lines, bend_above, left_above, total_above)
    blocks = [(left, bend_above), (left, bend_below), (left_above, bend_below)]
    sums[...] = pair_sums(plate, blocks, acc)


def stage_far(
    below, above, plate, left, bend_above, left_above,
    total, total_above, own_sums, near_sums,
    message,
    bend_far_below, left_far_below, bend_far_above, total_far_below, total_far_above,
    plain, cross, second, acc,
):
    lines = (plain, cross, second)
    stencil(below, plate, lines, bend_far_below, left_far_below, total_far_below)
    stencil(above, plate, lines, bend_far_above, None, total_far_above)
    blocks = [
        (left_above, bend_far_below), (left, bend_far_above),
        (left_far_below, bend_above), (left_far_below, bend_far_above),
    ]
    sums = pair_sums(plate, blocks, acc)
    owners, entries, _ = message.shape
    early = jnp.concatenate([near_sums[...], own_sums[...]], axis=1)
    message[:, :, 0:256] = early.reshape(owners, entries, 256)
    message[:, :, 256:512] = sums.reshape(owners, entries, 256)
    lane = lax.broadcasted_iota(jnp.int32, total.shape, 1)
    places = jnp.zeros(total.shape, f32)
    for place, panel in enumerate([total, total_above, total_far_above, total_far_below]):
        places = jnp.where(lane == place, panel[...], places)
    message[:, :, 512:640] = jnp.broadcast_to(places[None], (owners, entries, 128))


def three_parts(x):
    a = x.astype(bf16)
    rest = x - a.astype(f32)
    b = rest.astype(bf16)
    return a, b, (rest - b.astype(f32)).astype(bf16)


def gather_zones(received, lists, mine, to_far, to_next):
    places, width = received.shape
    zones = mine.shape[0]
    body = width - 128
    chosen = jnp.broadcast_to(lists[...], (zones, places)) == lax.broadcasted_iota(
        jnp.int32, (zones, places), 0
    )
    chosen = jnp.where(chosen, 1.0, 0.0).astype(bf16)
    zoned = sum(
        jnp.dot(chosen, part, preferred_element_type=f32) for part in three_parts(received[:, 0:body])
    )
    totals = jnp.sum(received[:, body:].reshape(places // 8, 8, 128), axis=0)
    mine[...] = zoned[:, 0:128]
    to_far[0:8, :] = totals
    to_far[8:, :] = zoned[:, 384:512]
    to_next[0:8, :] = totals
    to_next[8 : zones + 8, :] = zoned[:, 128:256]
    to_next[zones + 8 :, :] = zoned[:, 256:384]


def normalise(order, mine, kept, from_far, from_below, energy):
    zones = energy.shape[0]
    t = slice(0, 8)
    y = slice(8, zones + 8)
    z = slice(zones + 8, 2 * zones + 8)
    sums = jnp.concatenate(
        [
            kept[y, 64:128], mine[:, 0:64], kept[z, 64:128], from_far[y, 0:64],
            from_far[y, 64:128], from_below[z, 0:64], from_below[y, 0:64], mine[:, 64:128],
        ],
        axis=1,
    )
    own, far, below = kept[t, :], from_far[t, :], from_below[t, :]
    columns = [
        own[:, 0:1], own[:, 1:2], own[:, 2:3], far[:, 1:2],
        far[:, 2:3], below[:, 3:4], own[:, 3:4], below[:, 0:1],
    ]
    spread = jnp.concatenate([jnp.broadcast_to(c, (8, 64)) for c in columns], axis=1)
    sub = lax.broadcasted_iota(jnp.int32, (8, 512), 0)
    lane = lax.broadcasted_iota(jnp.int32, (8, 512), 1)
    total_j = jnp.sum(jnp.where((lane & 7) == sub, spread, 0.0), axis=0, keepdims=True)
    total_i = jnp.sum(
        jnp.where(((lane >> 3) & 7) == sub, jnp.broadcast_to(own[:, 0:1], (8, 512)), 0.0), axis=0, keepdims=True
    )
    scaled = ZONES * (0.5 * sums) / jnp.sqrt((0.5 * total_i) * (0.5 * total_j))
    parts = jnp.dot(jnp.concatenate(three_parts(scaled), axis=0), order[...], preferred_element_type=f32)
    ordered = parts[0:zones] + parts[zones : 2 * zones] + parts[2 * zones :]
    for i in range(8):
        energy[:, i, :] = ordered[:, i * 64 : (i + 1) * 64]


def vmem(shape, dtype=f32):
    return pltpu.VMEM(shape, dtype)


def call(body, outs, scratch, *args, spaces=()):
    where = list(spaces) + [pltpu.VMEM] * (len(args) - len(spaces))
    return pl.pallas_call(
        body,
        out_shape=[jax.ShapeDtypeStruct(s, d) for s, d in outs],
        in_specs=[pl.BlockSpec(memory_space=space) for space in where],
        out_specs=[pl.BlockSpec(memory_space=pltpu.VMEM)] * len(outs),
        scratch_shapes=scratch,
        compiler_params=pltpu.CompilerParams(vmem_limit_bytes=24 << 20),
    )(*args)


def per_device(mode_shapes, stiffness, node_slot, slot_zone):
    modes, rows, cells = mode_shapes.shape
    tiles = lax.axis_size("tile")
    panels = lax.axis_size("mode")
    entries = slot_zone.shape[2]
    slots = tiles * entries
    owned = ZONES // tiles
    up = [(i, i + 1) for i in range(tiles - 1)]
    down = [(i + 1, i) for i in range(tiles - 1)]

    def turn(x, by):
        return lax.ppermute(x, "mode", [(i, (i + by) % panels) for i in range(panels)])

    head = lax.ppermute(mode_shapes[:, rows - 1], "tile", up)
    tail = lax.ppermute(mode_shapes[:, 0], "tile", down)
    framed = jnp.concatenate([head[None], jnp.transpose(mode_shapes, (1, 0, 2)), tail[None]], axis=0)
    framed, rigid, named, places = lax.optimization_barrier((framed, stiffness, node_slot, slot_zone))
    plate = jnp.stack([rigid, named.astype(f32)])
    lists = lax.dynamic_index_in_dim(places, lax.axis_index("tile"), 1, keepdims=False).reshape(1, slots)
    plate, lists = lax.optimization_barrier((plate, lists))
    below = turn(framed, 1)
    above = turn(framed, -1)
    far_below = turn(below, 1)
    far_above = turn(above, -1)

    factor = ((3, rows, modes, cells), f32)
    total = ((modes, 128), f32)
    lines = [vmem((rows + 2, modes, cells))] * 3
    pairs = modes * modes
    place = lax.axis_index("mode").astype(jnp.int32).reshape(1)
    bend0, left0, total0, own_sums, order = call(
        stage_own, [factor, factor, total, ((slots, pairs), f32), ((8 * pairs, 8 * pairs), bf16)],
        lines + [vmem((2 * pairs, slots))],
        place, framed, plate, spaces=(pltpu.SMEM,),
    )
    bend_above, left_above, total_above, near_sums = call(
        stage_near, [factor, factor, total, ((slots, 3 * pairs), f32)],
        [vmem(*factor)] + lines + [vmem((6 * pairs, slots))],
        below, above, plate, bend0, left0,
    )
    (message,) = call(
        stage_far, [((tiles, entries, 8 * pairs + 128), f32)],
        [vmem(*factor)] * 3 + [vmem(*total)] * 2 + lines + [vmem((8 * pairs, slots))],
        far_below, far_above, plate, left0, bend_above, left_above,
        total0, total_above, own_sums, near_sums,
    )
    message, lists = lax.optimization_barrier((message, lists))
    received = lax.all_to_all(message, "tile", 0, 0, tiled=True)
    mine, to_far, to_next = call(
        gather_zones,
        [((owned, 128), f32), ((owned + 8, 128), f32), ((2 * owned + 8, 128), f32)], [],
        received.reshape(slots, 8 * pairs + 128), lists,
    )
    from_far = turn(to_far, -2)
    from_below = turn(to_next, 1)
    (energy,) = call(
        normalise, [((owned, modes, panels * modes), f32)], [],
        order, mine, to_next, from_far, from_below,
    )
    return energy


def solution(mesh):
    placed = (P("mode", "tile", None), P("tile", None), P("tile", None), P())

    return jax.shard_map(per_device, mesh=mesh, in_specs=placed, out_specs=P("tile", "mode", None), check_vma=False)
```
